32 devices in a mesh: row: 4 (over x, core), col: 8 (over z, y).
Axes of the slice: x: 2, y: 2, z: 4, core: 2. Of those that a mesh axis runs over, the one named last changes fastest.
Arguments:
- images: bfloat16 [64, 197, 384], P(('row', 'col')), may hold values from -6 to 6
- counts: int32 [32], replicated, may hold values from 1 to 2, 48 in all
- upstream: bfloat16 [64, 197, 384], P(('row', 'col')), may hold values from -6 to 6
- qkv_weight: float32 [442368], P(('row', 'col')), may hold values from -3 to 3, as said below
- out_weight: float32 [147456], P(('row', 'col')), may hold values from -1.75 to 1.75
- fc1_weight: float32 [589824], P(('row', 'col')), may hold values from -0.3125 to 0.3125
- fc2_weight: float32 [589824], P(('row', 'col')), may hold values from -0.15625 to 0.15625
- gains: float32 [768], P(('row', 'col')), may hold values from 0.1 to 1.9
- biases: float32 [3840], P(('row', 'col')), may hold values from -2 to 2
- first_qkv: float32 [442368], P(('row', 'col')), may hold values from -32 to 32
- first_out: float32 [147456], P(('row', 'col')), may hold values from -6 to 6
- first_fc1: float32 [589824], P(('row', 'col')), may hold values from -56 to 56
- first_fc2: float32 [589824], P(('row', 'col')), may hold values from -128 to 128
- first_gains: float32 [768], P(('row', 'col')), may hold values from -192 to 192
- first_biases: float32 [3840], P(('row', 'col')), may hold values from -96 to 96
- second_qkv: float32 [442368], P(('row', 'col')), may hold values from 67 to 667
- second_out: float32 [147456], P(('row', 'col')), may hold values from 13 to 67
- second_fc1: float32 [589824], P(('row', 'col')), may hold values from 170 to 830
- second_fc2: float32 [589824], P(('row', 'col')), may hold values from 830 to 4000
- second_gains: float32 [768], P(('row', 'col')), may hold values from 1700 to 8300
- second_biases: float32 [3840], P(('row', 'col')), may hold values from 330 to 6700
Outputs:
- block_out: bfloat16 [64, 197, 384], P(('row', 'col'))
- images_grad: bfloat16 [64, 197, 384], P(('row', 'col'))
- qkv_weight_grad: float32 [442368], P(('row', 'col'))
- out_weight_grad: float32 [147456], P(('row', 'col'))
- fc1_weight_grad: float32 [589824], P(('row', 'col'))
- fc2_weight_grad: float32 [589824], P(('row', 'col'))
- gains_grad: float32 [768], P(('row', 'col'))
- biases_grad: float32 [3840], P(('row', 'col'))
- qkv_weight_new: float32 [442368], P(('row', 'col'))
- out_weight_new: float32 [147456], P(('row', 'col'))
- fc1_weight_new: float32 [589824], P(('row', 'col'))
- fc2_weight_new: float32 [589824], P(('row', 'col'))
- gains_new: float32 [768], P(('row', 'col'))
- biases_new: float32 [3840], P(('row', 'col'))
- first_qkv_new: float32 [442368], P(('row', 'col'))
- first_out_new: float32 [147456], P(('row', 'col'))
- first_fc1_new: float32 [589824], P(('row', 'col'))
- first_fc2_new: float32 [589824], P(('row', 'col'))
- first_gains_new: float32 [768], P(('row', 'col'))
- first_biases_new: float32 [3840], P(('row', 'col'))
- second_qkv_new: float32 [442368], P(('row', 'col'))
- second_out_new: float32 [147456], P(('row', 'col'))
- second_fc1_new: float32 [589824], P(('row', 'col'))
- second_fc2_new: float32 [589824], P(('row', 'col'))
- second_gains_new: float32 [768], P(('row', 'col'))
- second_biases_new: float32 [3840], P(('row', 'col'))
The draws below stay inside these ranges and needn't reach their ends.
Inputs may be any that keep to these rules, and one draw needn't show every extreme that they name: `counts`: each device's entry is the number of its 2 image slots that hold images, the first ones; the entries sum to 48, and some device holds 2. `qkv_weight`: a dense projection matrix.
All inputs are finite; a program needn't handle non-finite values.
Results may differ from the reference program's by a relative error of at most 0.012.
The reference program's roundings to bfloat16 on the way count: a program that leaves them out, or rounds other values in their place, can miss the bound.
Values may be sent and summed in bfloat16 or wider, within the bound.
No kernel may reach another device: no remote copies, remote signals or barrier semaphores. Data moves between devices by JAX's collectives and lax.ppermute only.
A program may use at most 128 MiB of HBM per device.

```python
import math
import jax
import jax.numpy as jnp
import numpy as np
from jax import lax

D = 384
HEADS = 6
HEAD_DIM = 64
FF = 1536
SEQ = 197
ADAM_STEP = 3
IMG_DEV = 2
SLOTS = 64
IMAGES = 48
DEVICES = 32


def draw_qkv_weight(key, part):
    base_draw = jax.random.normal(key, (D, 3 * D), jnp.float32) * D ** (-0.5)
    full_draw = base_draw
    return full_draw.reshape(-1)


def shard_levels(rng, dims, split, low, high):
    level, own = 1.0, jax.random.fold_in(rng, 6)
    for dim, shards_of in split:
        heights = jnp.exp(jax.random.uniform(jax.random.fold_in(own, dim), (shards_of,), jnp.float32, low / len(split), high / len(split)))
        level = level * jnp.repeat(heights, dims[dim] // shards_of).reshape([-1 if axis == dim else 1 for axis in range(len(dims))])
    return level


def split_up(amount, total, reach, lean):
    weights = [(1 << 20) // math.isqrt(grade ** lean) + 1 for grade in range(2, amount + 1)]
    rest, holding = total - reach - (amount - 1), [1] * (amount - 1)
    while rest > 0:
        movable = [i for i in range(amount - 1) if holding[i] < reach]
        pool, remaining = sum([weights[i] for i in movable]), rest
        for i in movable:
            more = min(reach - holding[i], max(1, remaining * weights[i] // pool), rest)
            holding[i] = holding[i] + more
            rest = rest - more
    return np.array([reach] + holding)


def ragged(rng, count, total, bound, lean):
    if count == 2:
        one = jax.random.randint(rng, (), max(1, total - bound), min(bound, total - 1) + 1)
        return jnp.stack([one, total - one])
    sizes = jnp.asarray(split_up(count, total, bound, lean), jnp.int32)
    couples = (count - 1) // 2
    donor, sink = sizes[1:1 + 2 * couples:2], sizes[2:2 + 2 * couples:2]
    room = jnp.minimum(donor - 1, bound - sink)
    shifted = jax.random.randint(jax.random.fold_in(rng, 1), (couples,), 0, 1 << 20) % (room + 1)
    sizes = sizes.at[1:1 + 2 * couples:2].set(donor - shifted).at[2:2 + 2 * couples:2].set(sink + shifted)
    return sizes[jax.random.permutation(jax.random.fold_in(rng, 2), count)]


def normal_values(stream_key, shape, scale, reach, shards=(), kind=jnp.bfloat16):
    drawn = jax.random.normal(stream_key, shape, jnp.float32) * scale
    if len(shards) > 0:
        drawn = shard_levels(stream_key, shape, shards, -0.22, 0.18) * drawn
    return jnp.clip(drawn, min=-reach, max=reach).astype(kind)


def setup_inputs(seed: int = 0) -> dict:
    key_of = jax.random.split(jax.random.key(seed), 22)
    images = normal_values(key_of[0], (SLOTS, SEQ, D), 1.0, 6.0, ((0, 32),))
    counts = ragged(key_of[1], DEVICES, IMAGES, IMG_DEV, 2).astype(jnp.int32)
    upstream = normal_values(key_of[2], (SLOTS, SEQ, D), 1.0, 6.0, ((0, 32),))
    qkv_weight = draw_qkv_weight(jax.random.fold_in(key_of[21], 71), 0)
    out_weight = normal_values(key_of[4], (D * D,), (D // 32) ** -0.5, 1.75, ((0, 32),), jnp.float32)
    fc1_weight = normal_values(key_of[5], (D * FF,), D ** -0.5, 0.3125, ((0, 32),), jnp.float32)
    fc2_weight = normal_values(key_of[6], (FF * D,), FF ** -0.5, 0.15625, ((0, 32),), jnp.float32)
    gains = jnp.clip(1.0 + 0.18 * jax.random.normal(key_of[7], (2 * D,), jnp.float32), 0.1, 1.9)
    biases = normal_values(key_of[8], (6 * D + FF,), 0.3, 2.0, ((0, 32),), jnp.float32)
    first_qkv = normal_values(key_of[9], (3 * D * D,), 6.0, 32.0, ((0, 32),), jnp.float32)
    first_out = normal_values(key_of[10], (D * D,), 2.3, 6.0, ((0, 32),), jnp.float32)
    first_fc1 = normal_values(key_of[11], (D * FF,), 9.0, 56.0, ((0, 32),), jnp.float32)
    first_fc2 = normal_values(key_of[12], (FF * D,), 20.0, 128.0, ((0, 32),), jnp.float32)
    first_gains = normal_values(key_of[13], (2 * D,), 30.0, 192.0, ((0, 32),), jnp.float32)
    first_biases = normal_values(key_of[14], (6 * D + FF,), 17.0, 96.0, ((0, 32),), jnp.float32)
    second_qkv = jnp.clip(jnp.exp(math.log(667.0) - 2.2980974 * jax.random.uniform(key_of[15], (3 * D * D,), jnp.float32) ** shard_levels(key_of[15], (3 * D * D,), ((0, 32),), -0.2, 0.2)), 67.0, 667.0)
    second_out = jnp.clip(jnp.exp(math.log(67.0) - 1.63974326 * jax.random.uniform(key_of[16], (D * D,), jnp.float32) ** shard_levels(key_of[16], (D * D,), ((0, 32),), -0.2, 0.2)), 13.0, 67.0)
    second_fc1 = jnp.clip(jnp.exp(math.log(830.0) - 1.5856273 * jax.random.uniform(key_of[17], (D * FF,), jnp.float32) ** shard_levels(key_of[17], (D * FF,), ((0, 32),), -0.2, 0.2)), 170.0, 830.0)
    second_fc2 = jnp.clip(jnp.exp(math.log(4000.0) - 1.572624 * jax.random.uniform(key_of[18], (FF * D,), jnp.float32) ** shard_levels(key_of[18], (FF * D,), ((0, 32),), -0.2, 0.2)), 830.0, 4000.0)
    second_gains = jnp.clip(jnp.exp(math.log(8300.0) - 1.5856273 * jax.random.uniform(key_of[19], (2 * D,), jnp.float32) ** shard_levels(key_of[19], (2 * D,), ((0, 32),), -0.2, 0.2)), 1700.0, 8300.0)
    second_biases = jnp.clip(jnp.exp(math.log(6700.0) - 3.01077 * jax.random.uniform(key_of[20], (6 * D + FF,), jnp.float32) ** shard_levels(key_of[20], (6 * D + FF,), ((0, 32),), -0.2, 0.2)), 330.0, 6700.0)
    return dict(images=images, counts=counts, upstream=upstream, qkv_weight=qkv_weight, out_weight=out_weight, fc1_weight=fc1_weight, fc2_weight=fc2_weight, gains=gains, biases=biases, first_qkv=first_qkv, first_out=first_out, first_fc1=first_fc1, first_fc2=first_fc2, first_gains=first_gains, first_biases=first_biases, second_qkv=second_qkv, second_out=second_out, second_fc1=second_fc1, second_fc2=second_fc2, second_gains=second_gains, second_biases=second_biases)


NORM_EPS = 1e-06
BETA_ONE = 0.9
BETA_TWO = 0.95
ADAM_EPS = 1e-08
DECAY_RATE = 0.1
RATES = (0.01, 0.05, 0.01, 0.01, 0.2, 0.2)
DECAYED = (True, True, True, True, False, False)
INV_ROOT_TWO = 0.7071067811865476
INV_ROOT_TWOPI = 0.3989422804014327

def unpack_params(flat_params):
    qkv_flat, out_flat, fc1_flat, fc2_flat, gain_flat, bias_flat = flat_params
    gain_vals = gain_flat.astype(jnp.float32)
    bias_vals = bias_flat.astype(jnp.float32)
    return (qkv_flat.reshape(D, 3 * D), out_flat.reshape(D, D), fc1_flat.reshape(D, FF), fc2_flat.reshape(FF, D), gain_vals[:D], gain_vals[D:], bias_vals[:D], bias_vals[D:2 * D], bias_vals[2 * D:3 * D], bias_vals[3 * D:4 * D], bias_vals[4 * D:5 * D], bias_vals[5 * D:5 * D + FF], bias_vals[5 * D + FF:])

def norm_forward(row_data):
    centered = row_data - lax.optimization_barrier(jnp.mean(row_data, axis=-1, keepdims=True))
    inv_std = lax.rsqrt(lax.optimization_barrier(jnp.mean(centered * centered, axis=-1, keepdims=True)) + NORM_EPS)
    return (centered * inv_std, inv_std)

def norm_backward(grad_hat, normed, inv_std):
    return inv_std * (grad_hat - lax.optimization_barrier(jnp.mean(grad_hat, axis=-1, keepdims=True)) - normed * lax.optimization_barrier(jnp.mean(grad_hat * normed, axis=-1, keepdims=True)))

def attention_scores(queries, key_rows):
    return jnp.einsum('bqhe,bkhe->bhqk', queries.astype(jnp.float32), key_rows.astype(jnp.float32)) * HEAD_DIM ** (-0.5)

def block_grads(images_block, grad_block, live_block, params):
    w_qkv, w_out, w_fc1, w_fc2, gain_one, gain_two, shift_one, query_bias, value_bias, out_bias, shift_two, fc1_bias, fc2_bias = params
    batch_size = images_block.shape[0]
    row_count = batch_size * SEQ
    x_float = images_block.reshape(row_count, D).astype(jnp.float32)
    hat_in, inv_in = norm_forward(x_float)
    normed_in = (hat_in * gain_one + shift_one).astype(jnp.bfloat16)
    projected = jnp.dot(normed_in, w_qkv, preferred_element_type=jnp.float32)
    queries = (projected[:, :D] + query_bias).astype(jnp.bfloat16).reshape(batch_size, SEQ, HEADS, HEAD_DIM)
    key_rows = projected[:, D:2 * D].astype(jnp.bfloat16).reshape(batch_size, SEQ, HEADS, HEAD_DIM)
    value_rows = (projected[:, 2 * D:] + value_bias).astype(jnp.bfloat16).reshape(batch_size, SEQ, HEADS, HEAD_DIM)
    scores = attention_scores(queries, key_rows)
    row_max = lax.optimization_barrier(jnp.max(scores, axis=-1, keepdims=True))
    log_total = row_max + jnp.log(lax.optimization_barrier(jnp.sum(jnp.exp(scores - row_max), axis=-1, keepdims=True)))
    probs_bf = jnp.exp(scores - log_total).astype(jnp.bfloat16)
    attended_heads = jnp.einsum('bhqk,bkhe->bqhe', probs_bf.astype(jnp.float32), value_rows.astype(jnp.float32)).astype(jnp.bfloat16)
    attended = attended_heads.reshape(row_count, D)
    mid_stream = x_float + jnp.dot(attended, w_out, preferred_element_type=jnp.float32) + out_bias
    hat_mid, inv_mid = norm_forward(mid_stream)
    normed_mid = (hat_mid * gain_two + shift_two).astype(jnp.bfloat16)
    hidden_pre = jnp.dot(normed_mid, w_fc1, preferred_element_type=jnp.float32) + fc1_bias
    hidden_act = jax.nn.gelu(hidden_pre, approximate=False).astype(jnp.bfloat16)
    result = mid_stream + jnp.dot(hidden_act, w_fc2, preferred_element_type=jnp.float32) + fc2_bias
    live_rows = jnp.repeat(live_block, SEQ)[:, None]
    block_out = (result * live_rows).astype(jnp.bfloat16).reshape(batch_size, SEQ, D)
    grad_out = (grad_block.reshape(row_count, D).astype(jnp.float32) * live_rows).astype(jnp.bfloat16)
    grad_float = grad_out.astype(jnp.float32)
    grad_fc2 = jnp.dot(hidden_act.T, grad_out, preferred_element_type=jnp.float32)
    grad_act = jnp.dot(grad_out, w_fc2.T, preferred_element_type=jnp.float32)
    gelu_slope = 0.5 * (1.0 + lax.erf(hidden_pre * INV_ROOT_TWO)) + hidden_pre * INV_ROOT_TWOPI * jnp.exp(-0.5 * hidden_pre * hidden_pre)
    grad_pre = grad_act * gelu_slope
    grad_pre_bf = grad_pre.astype(jnp.bfloat16)
    grad_fc1 = jnp.dot(normed_mid.T, grad_pre_bf, preferred_element_type=jnp.float32)
    grad_normed = jnp.dot(grad_pre_bf, w_fc1.T, preferred_element_type=jnp.float32)
    grad_mid = grad_float + norm_backward(grad_normed * gain_two, hat_mid, inv_mid)
    grad_mid_bf = grad_mid.astype(jnp.bfloat16)
    grad_outproj = jnp.dot(attended.T, grad_mid_bf, preferred_element_type=jnp.float32)
    grad_attended = jnp.dot(grad_mid_bf, w_out.T, preferred_element_type=jnp.float32).astype(jnp.bfloat16).reshape(batch_size, SEQ, HEADS, HEAD_DIM)
    scores_again = attention_scores(queries, key_rows)
    probs = jnp.exp(scores_again - log_total)
    probs_again = probs.astype(jnp.bfloat16)
    grad_values = jnp.einsum('bhqk,bqhe->bkhe', probs_again.astype(jnp.float32), grad_attended.astype(jnp.float32))
    grad_probs = jnp.einsum('bqhe,bkhe->bhqk', grad_attended.astype(jnp.float32), value_rows.astype(jnp.float32))
    row_dot = lax.optimization_barrier(jnp.sum(grad_attended.astype(jnp.float32) * attended_heads.astype(jnp.float32), axis=-1))
    row_dot = jnp.transpose(row_dot, (0, 2, 1))[..., None]
    grad_scores = (probs * (grad_probs - row_dot) * HEAD_DIM ** (-0.5)).astype(jnp.bfloat16)
    grad_queries = jnp.einsum('bhqk,bkhe->bqhe', grad_scores.astype(jnp.float32), key_rows.astype(jnp.float32)).reshape(row_count, D)
    grad_keys = jnp.einsum('bhqk,bqhe->bkhe', grad_scores.astype(jnp.float32), queries.astype(jnp.float32)).reshape(row_count, D)
    grad_values = grad_values.reshape(row_count, D)
    grad_proj = jnp.concatenate([grad_queries, grad_keys, grad_values], axis=1).astype(jnp.bfloat16)
    grad_qkv = jnp.dot(normed_in.T, grad_proj, preferred_element_type=jnp.float32)
    grad_normed_in = jnp.dot(grad_proj, w_qkv.T, preferred_element_type=jnp.float32)
    images_grad = (grad_mid + norm_backward(grad_normed_in * gain_one, hat_in, inv_in)).astype(jnp.bfloat16).reshape(batch_size, SEQ, D)
    grad_gains = jnp.concatenate([lax.optimization_barrier(jnp.sum(grad_normed_in * hat_in, axis=0)), lax.optimization_barrier(jnp.sum(grad_normed * hat_mid, axis=0))])
    grad_biases = jnp.concatenate([lax.optimization_barrier(jnp.sum(grad_normed_in, axis=0)), lax.optimization_barrier(jnp.sum(grad_queries, axis=0)), lax.optimization_barrier(jnp.sum(grad_values, axis=0)), lax.optimization_barrier(jnp.sum(grad_mid, axis=0)), lax.optimization_barrier(jnp.sum(grad_normed, axis=0)), lax.optimization_barrier(jnp.sum(grad_pre, axis=0)), lax.optimization_barrier(jnp.sum(grad_float, axis=0))])
    grads = (grad_qkv.reshape(-1), grad_outproj.reshape(-1), grad_fc1.reshape(-1), grad_fc2.reshape(-1), grad_gains, grad_biases)
    return (block_out, images_grad, grads)

def adam_update(weight, gradient, moment_one, moment_two, step_rate, decayed):
    first_new = BETA_ONE * moment_one + (1.0 - BETA_ONE) * gradient
    second_new = BETA_TWO * moment_two + (1.0 - BETA_TWO) * gradient * gradient
    first_hat = first_new / (1.0 - BETA_ONE ** ADAM_STEP)
    second_hat = second_new / (1.0 - BETA_TWO ** ADAM_STEP)
    change = first_hat / (jnp.sqrt(second_hat) + ADAM_EPS)
    if decayed:
        change = change + DECAY_RATE * weight
    return (weight - step_rate * change, first_new, second_new)

def reference(images, counts, upstream, qkv_weight, out_weight, fc1_weight, fc2_weight, gains, biases, first_qkv, first_out, first_fc1, first_fc2, first_gains, first_biases, second_qkv, second_out, second_fc1, second_fc2, second_gains, second_biases):
    masters = (qkv_weight, out_weight, fc1_weight, fc2_weight, gains, biases)
    firsts = (first_qkv, first_out, first_fc1, first_fc2, first_gains, first_biases)
    seconds = (second_qkv, second_out, second_fc1, second_fc2, second_gains, second_biases)
    params = unpack_params(tuple((master.astype(jnp.bfloat16) for master in masters)))
    slot_ids = jnp.arange(SLOTS, dtype=jnp.int32)
    live_mask = (slot_ids % IMG_DEV < counts[slot_ids // IMG_DEV]).astype(jnp.float32)
    block_size = 4 * IMG_DEV
    blocks = SLOTS // block_size

    def step_fn(running, inputs):
        images_block, grad_block, live_block = inputs
        out_block, input_block, grads = block_grads(images_block, grad_block, live_block, params)
        return (tuple((total + piece for total, piece in zip(running, grads))), (out_block, input_block))
    zero_grads = tuple((jnp.zeros(master.shape, jnp.float32) for master in masters))
    totals, (block_outs, input_grads) = lax.scan(step_fn, zero_grads, (images.reshape(blocks, block_size, SEQ, D), upstream.reshape(blocks, block_size, SEQ, D), live_mask.reshape(blocks, block_size)))
    block_out = block_outs.reshape(SLOTS, SEQ, D)
    images_grad = input_grads.reshape(SLOTS, SEQ, D)
    new_weights = []
    new_firsts = []
    new_seconds = []
    for position in range(6):
        weight_new, first_new, second_new = adam_update(masters[position], totals[position], firsts[position], seconds[position], RATES[position], DECAYED[position])
        new_weights.append(weight_new)
        new_firsts.append(first_new)
        new_seconds.append(second_new)
    return (block_out, images_grad, totals[0], totals[1], totals[2], totals[3], totals[4], totals[5], new_weights[0], new_weights[1], new_weights[2], new_weights[3], new_weights[4], new_weights[5], new_firsts[0], new_firsts[1], new_firsts[2], new_firsts[3], new_firsts[4], new_firsts[5], new_seconds[0], new_seconds[1], new_seconds[2], new_seconds[3], new_seconds[4], new_seconds[5])
```

```python
import math

import jax
import jax.numpy as jnp
from jax import lax
from jax.experimental import pallas as pl
from jax.experimental.pallas import tpu as pltpu
from jax.sharding import PartitionSpec as P

D = 384
HEADS = 6
HEAD_DIM = 64
FF = 1536
SEQ = 197
ADAM_STEP = 3

NORM_EPS = 1e-06
BETA_ONE = 0.9
BETA_TWO = 0.95
ADAM_EPS = 1e-08
DECAY_RATE = 0.1
RATES = (0.01, 0.05, 0.01, 0.01, 0.2, 0.2)
DECAYED = (True, True, True, True, False, False)
INV_ROOT_TWO = 0.7071067811865476
INV_ROOT_TWOPI = 0.3989422804014327

AXES = ("row", "col")
F32 = jnp.float32
BF16 = jnp.bfloat16
LANES = 128
PAD = 208
IMGS = 2
ROWS = IMGS * PAD
BLOCKS = 32
STRIPE = D // BLOCKS
QKV_TILES = 3 * D // LANES
OUT_TILES = D // LANES
FC_TILES = FF // LANES
QKV_ROWS = STRIPE * QKV_TILES
OUT_ROWS = STRIPE * OUT_TILES
FC_ROWS = STRIPE * FC_TILES
TALL = FF // BLOCKS
FIRST_ROWS = 160
FIRST_HALF = 80
SECOND_ROWS = 2 * FC_ROWS
BIAS_ROW = QKV_ROWS + OUT_ROWS
GAIN_ROW = BIAS_ROW + 1
GAINS = 2 * D
BIASES = 6 * D + FF
GAIN_PART = GAINS // BLOCKS
BIAS_PART = BIASES // BLOCKS
CHUNKS = FF // D
Y_BIT, Z_LOW, Z_HIGH, CORE_BIT, X_BIT = 1, 2, 4, 8, 16


def nn(a, b):
    return jnp.dot(a, b, preferred_element_type=F32)


def nt(a, b):
    return lax.dot_general(a, b, (((1,), (1,)), ((), ())), preferred_element_type=F32)


def tn(a, b):
    return lax.dot_general(a, b, (((0,), (0,)), ((), ())), preferred_element_type=F32)


def norm_forward(row_data):
    centered = row_data - jnp.mean(row_data, axis=-1, keepdims=True)
    inv_std = lax.rsqrt(jnp.mean(centered * centered, axis=-1, keepdims=True) + NORM_EPS)
    return (centered * inv_std, inv_std)


def norm_backward(grad_hat, normed, inv_std):
    return inv_std * (
        grad_hat
        - jnp.mean(grad_hat, axis=-1, keepdims=True)
        - normed * jnp.mean(grad_hat * normed, axis=-1, keepdims=True)
    )


def masks_of(index, color):
    return (index & 3) * Z_LOW + (index >> 2) * (Y_BIT if color == 0 else X_BIT)


def variants(color):
    last = X_BIT if color == 0 else Y_BIT
    return (0, last, CORE_BIT, last + CORE_BIT)


def unpack(me, piece_refs, flat_ref, color, start, count):
    for piece_ref, extra in zip(piece_refs, variants(color)):

        def body(i, carry, piece_ref=piece_ref, extra=extra):
            owner = me ^ (masks_of(i, color) ^ extra)
            flat_ref[owner, start : start + count, :] = piece_ref[i].astype(F32)
            return carry

        lax.fori_loop(0, 8, body, 0)


def pack(me, grad_ref, out_refs, color, start, count):
    for out_ref, extra in zip(out_refs, variants(color)):

        def body(i, carry, out_ref=out_ref, extra=extra):
            owner = me ^ (masks_of(i, color) ^ extra)
            out_ref[i] = grad_ref[owner, start : start + count, :].astype(BF16)
            return carry

        lax.fori_loop(0, 8, body, 0)


def striped_rows(flat_ref, quad, start, stride):
    parts = [flat_ref[4 * quad + u, pl.ds(start, STRIPE, stride=stride), :] for u in range(4)]
    return jnp.concatenate(parts, axis=0).astype(BF16)


def select_matrix(part, total):
    lane = lax.broadcasted_iota(jnp.int32, (LANES, total), 1)
    sub = lax.broadcasted_iota(jnp.int32, (LANES, total), 0)
    block = (lane * ((1 << 22) // part + 1)) >> 22
    return jnp.where(lane - block * part == sub, 1.0, 0.0).astype(BF16)


def owner_mask(part, total):
    lane = lax.broadcasted_iota(jnp.int32, (BLOCKS, total), 1)
    block = lax.broadcasted_iota(jnp.int32, (BLOCKS, total), 0)
    return (lane >= block * part) & (lane < block * part + part)


def spread(block_rows, part, total):
    moved = nn(block_rows.astype(BF16), select_matrix(part, total))
    return jnp.sum(jnp.where(owner_mask(part, total), moved, 0.0), axis=0, keepdims=True)


def collect(row, part, total):
    own = jnp.where(owner_mask(part, total), jnp.broadcast_to(row, (BLOCKS, total)), 0.0)
    return nt(own.astype(BF16), select_matrix(part, total))


def load_padded(x_ref, padded_ref, scales=None):
    for b in range(IMGS):
        tail = (SEQ // 16) * 16
        padded_ref[b * PAD + tail : (b + 1) * PAD, :] = jnp.zeros((PAD - tail, D), F32)
        value = x_ref[b].astype(F32)
        if scales is not None:
            value = value * scales[b]
        padded_ref[b * PAD : b * PAD + SEQ, :] = value


def bias_slice(vec_ref, start, size):
    return vec_ref[:, GAINS + start : GAINS + start + size]


def head_masks():
    lane = lax.broadcasted_iota(jnp.int32, (1, LANES), 1)
    low = jnp.where(lane < HEAD_DIM, 1.0, 0.0)
    return (low.astype(BF16), (1.0 - low).astype(BF16))


def attend_kernel(info_ref, x_ref, *refs):
    pieces = refs[:8]
    wqkv_ref, wout_ref, vec_ref, qkv_ref, att_ref = refs[8:13]
    flat_ref, pad_ref = refs[13:]
    me = info_ref[0]
    unpack(me, pieces[:4], flat_ref, 0, 0, FIRST_HALF)
    unpack(me, pieces[4:], flat_ref, 1, FIRST_HALF, FIRST_HALF)

    def quads(quad, carry):
        rows = pl.ds(pl.multiple_of(quad * 4 * STRIPE, 16), 4 * STRIPE)
        for t in range(QKV_TILES):
            wqkv_ref[rows, t * LANES : (t + 1) * LANES] = striped_rows(
                flat_ref, quad, t, QKV_TILES
            )
        for t in range(OUT_TILES):
            wout_ref[rows, t * LANES : (t + 1) * LANES] = striped_rows(
                flat_ref, quad, QKV_ROWS + t, OUT_TILES
            )
        return carry

    lax.fori_loop(0, BLOCKS // 4, quads, 0)
    vec_ref[:, :GAINS] = spread(flat_ref[:, GAIN_ROW, :], GAIN_PART, GAINS)
    vec_ref[:, GAINS:] = spread(flat_ref[:, BIAS_ROW, :], BIAS_PART, BIASES)

    load_padded(x_ref, pad_ref)
    hat_in, _ = norm_forward(pad_ref[...])
    normed_in = (hat_in * vec_ref[:, :D] + bias_slice(vec_ref, 0, D)).astype(BF16)
    qkv_ref[:, :D] = (
        nn(normed_in, wqkv_ref[:, :D]) + bias_slice(vec_ref, D, D)
    ).astype(BF16)
    qkv_ref[:, D : 2 * D] = nn(normed_in, wqkv_ref[:, D : 2 * D]).astype(BF16)
    qkv_ref[:, 2 * D :] = (
        nn(normed_in, wqkv_ref[:, 2 * D :]) + bias_slice(vec_ref, 2 * D, D)
    ).astype(BF16)

    masks = head_masks()
    lane = lax.broadcasted_iota(jnp.int32, (1, LANES), 1)
    dead = jnp.where(lax.broadcasted_iota(jnp.int32, (1, PAD), 1) < SEQ, 0.0, -1e30)

    def image(b, carry):
        rows = pl.ds(pl.multiple_of(b * PAD, 16), PAD)
        for pair in range(HEADS // 2):
            cols = pair * LANES
            q2 = qkv_ref[rows, cols : cols + LANES]
            k2 = qkv_ref[rows, D + cols : D + cols + LANES]
            v2 = qkv_ref[rows, 2 * D + cols : 2 * D + cols + LANES]
            outs = []
            for mask in masks:
                scores = nt(q2 * mask, k2) * HEAD_DIM ** (-0.5) + dead
                top = jnp.max(scores, axis=-1, keepdims=True)
                grown = jnp.exp(scores - top)
                total = jnp.sum(grown, axis=-1, keepdims=True)
                probs = (grown * (1.0 / total)).astype(BF16)
                outs.append(nn(probs, v2))
            att_ref[rows, cols : cols + LANES] = jnp.where(
                lane < HEAD_DIM, outs[0], outs[1]
            ).astype(BF16)
        return carry

    lax.fori_loop(0, IMGS, image, 0)


def mlp_kernel(info_ref, x_ref, up_ref, att_ref, wout_ref, vec_ref, *refs):
    pieces = refs[:8]
    out_ref, gmid_ref, vecg_ref = refs[8:11]
    grads = refs[11:19]
    flat1, flat2, w1, w2, dw1, dw2, b1, b1g, pad_ref, go_ref, nm_ref, acc, gacc = refs[19:]
    me = info_ref[0]
    live = [jnp.where(info_ref[1] > b, 1.0, 0.0).astype(F32) for b in range(IMGS)]
    unpack(me, pieces[:4], flat1, 0, 0, FC_ROWS)
    unpack(me, pieces[4:], flat2, 1, 0, FC_ROWS)

    def quads(quad, carry):
        rows = pl.ds(pl.multiple_of(quad * 4 * STRIPE, 16), 4 * STRIPE)
        for t in range(FC_TILES):
            w1[t // 3, rows, (t % 3) * LANES : (t % 3 + 1) * LANES] = striped_rows(
                flat1, quad, t, FC_TILES
            )
        return carry

    lax.fori_loop(0, BLOCKS // 4, quads, 0)

    def talls(d, carry):
        rows = pl.ds(pl.multiple_of((d & 7) * TALL, 16), TALL)
        for t in range(OUT_TILES):
            w2[d >> 3, rows, t * LANES : (t + 1) * LANES] = flat2[
                d, pl.ds(t, TALL, stride=OUT_TILES), :
            ].astype(BF16)
        return carry

    lax.fori_loop(0, BLOCKS, talls, 0)
    for j in range(CHUNKS):
        b1[j] = bias_slice(vec_ref, 5 * D + j * D, D)

    load_padded(x_ref, pad_ref)
    load_padded(up_ref, acc, live)
    go_ref[...] = acc[...].astype(BF16)
    mid = pad_ref[...] + nn(att_ref[...], wout_ref[...]) + bias_slice(vec_ref, 3 * D, D)
    hat_mid, inv_mid = norm_forward(mid)
    nm_ref[...] = (hat_mid * vec_ref[:, D : 2 * D] + bias_slice(vec_ref, 4 * D, D)).astype(BF16)
    acc[...] = mid + bias_slice(vec_ref, 5 * D + FF, D)
    pad_ref[...] = mid
    gacc[...] = jnp.zeros((ROWS, D), F32)

    def chunk(j, carry):
        hidden = nn(nm_ref[...], w1[j]) + b1[j]
        cdf = 0.5 * (1.0 + lax.erf(hidden * INV_ROOT_TWO))
        act = (hidden * cdf).astype(BF16)
        slope = cdf + hidden * INV_ROOT_TWOPI * jnp.exp(-0.5 * hidden * hidden)
        acc[...] += nn(act, w2[j])
        dw2[j] = tn(act, go_ref[...])
        grad_pre = nt(go_ref[...], w2[j]) * slope
        b1g[j] = jnp.sum(grad_pre, axis=0, keepdims=True)
        grad_pre_bf = grad_pre.astype(BF16)
        dw1[j] = tn(nm_ref[...], grad_pre_bf)
        gacc[...] += nt(grad_pre_bf, w1[j])
        return carry

    lax.fori_loop(0, CHUNKS, chunk, 0)
    for b in range(IMGS):
        out_ref[b] = (acc[b * PAD : b * PAD + SEQ, :] * live[b]).astype(BF16)

    hat_mid, inv_mid = norm_forward(pad_ref[...])
    grad_normed = gacc[...]
    grad_float = go_ref[...].astype(F32)
    grad_mid = grad_float + norm_backward(grad_normed * vec_ref[:, D : 2 * D], hat_mid, inv_mid)
    gmid_ref[...] = grad_mid
    vecg_ref[...] = jnp.zeros((1, GAINS + BIASES), F32)
    vecg_ref[:, D : 2 * D] = jnp.sum(grad_normed * hat_mid, axis=0, keepdims=True)
    base = GAINS
    vecg_ref[:, base + 3 * D : base + 4 * D] = jnp.sum(grad_mid, axis=0, keepdims=True)
    vecg_ref[:, base + 4 * D : base + 5 * D] = jnp.sum(grad_normed, axis=0, keepdims=True)
    for j in range(CHUNKS):
        vecg_ref[:, base + (5 + j) * D : base + (6 + j) * D] = b1g[j]
    vecg_ref[:, base + 5 * D + FF :] = jnp.sum(grad_float, axis=0, keepdims=True)

    def pairs(p, carry):
        rows = pl.ds(pl.multiple_of(p * 2 * STRIPE, 8), 2 * STRIPE)
        for t in range(FC_TILES):
            value = dw1[t // 3, rows, (t % 3) * LANES : (t % 3 + 1) * LANES]
            for u in range(2):
                flat1[2 * p + u, pl.ds(t, STRIPE, stride=FC_TILES), :] = value[
                    u * STRIPE : (u + 1) * STRIPE
                ]
        return carry

    lax.fori_loop(0, BLOCKS // 2, pairs, 0)

    def talls_back(d, carry):
        rows = pl.ds(pl.multiple_of((d & 7) * TALL, 16), TALL)
        for t in range(OUT_TILES):
            flat2[d, pl.ds(t, TALL, stride=OUT_TILES), :] = dw2[
                d >> 3, rows, t * LANES : (t + 1) * LANES
            ]
        return carry

    lax.fori_loop(0, BLOCKS, talls_back, 0)
    pack(me, flat1, grads[:4], 0, 0, FC_ROWS)
    pack(me, flat2, grads[4:], 1, 0, FC_ROWS)


def back_kernel(
    info_ref, x_ref, qkv_ref, att_ref, gmid_ref, wqkv_ref, wout_ref, vec_ref, vecg_ref, *refs
):
    xgrad_ref = refs[0]
    grads = refs[1:9]
    flat_ref, pad_ref, ga_ref, gp_ref, gpb_ref, dwq, dwo, vsum = refs[9:]
    me = info_ref[0]
    gmid_bf = gmid_ref[...].astype(BF16)
    ga_ref[...] = nt(gmid_bf, wout_ref[...]).astype(BF16)
    dwo[...] = tn(att_ref[...], gmid_bf)

    masks = head_masks()
    alive = jnp.where(lax.broadcasted_iota(jnp.int32, (PAD, 1), 0) < SEQ, 0.0, -1e30)

    def image(b, carry):
        rows = pl.ds(pl.multiple_of(b * PAD, 16), PAD)
        for pair in range(HEADS // 2):
            cols = pair * LANES
            q2 = qkv_ref[rows, cols : cols + LANES]
            k2 = qkv_ref[rows, D + cols : D + cols + LANES]
            v2 = qkv_ref[rows, 2 * D + cols : 2 * D + cols + LANES]
            g2 = ga_ref[rows, cols : cols + LANES]
            gq = jnp.zeros((PAD, LANES), F32)
            gk = jnp.zeros((PAD, LANES), F32)
            gv = jnp.zeros((PAD, LANES), F32)
            for mask in masks:
                qm = q2 * mask
                gm = g2 * mask
                scores = nt(k2, qm) * HEAD_DIM ** (-0.5) + alive
                top = jnp.max(scores, axis=0, keepdims=True)
                grown = jnp.exp(scores - top)
                total = jnp.sum(grown, axis=0, keepdims=True)
                probs = grown * (1.0 / total)
                grad_probs = nt(v2, gm)
                row_dot = jnp.sum(probs * grad_probs, axis=0, keepdims=True)
                grad_scores = (probs * (grad_probs - row_dot) * HEAD_DIM ** (-0.5)).astype(BF16)
                gv = gv + nn(probs.astype(BF16), gm)
                gk = gk + nn(grad_scores, qm)
                gq = gq + tn(grad_scores, k2 * mask)
            gp_ref[rows, cols : cols + LANES] = gq
            gp_ref[rows, D + cols : D + cols + LANES] = gk
            gp_ref[rows, 2 * D + cols : 2 * D + cols + LANES] = gv
        return carry

    lax.fori_loop(0, IMGS, image, 0)

    load_padded(x_ref, pad_ref)
    hat_in, inv_in = norm_forward(pad_ref[...])
    normed_in = (hat_in * vec_ref[:, :D] + bias_slice(vec_ref, 0, D)).astype(BF16)
    gpb_ref[...] = gp_ref[...].astype(BF16)
    dwq[...] = tn(normed_in, gpb_ref[...])
    grad_in = nt(gpb_ref[...], wqkv_ref[...])
    images_grad = gmid_ref[...] + norm_backward(grad_in * vec_ref[:, :D], hat_in, inv_in)
    pad_ref[...] = images_grad
    for b in range(IMGS):
        xgrad_ref[b] = pad_ref[b * PAD : b * PAD + SEQ, :].astype(BF16)

    vsum[...] = vecg_ref[...]
    vsum[:, :D] = jnp.sum(grad_in * hat_in, axis=0, keepdims=True)
    vsum[:, GAINS : GAINS + D] = jnp.sum(grad_in, axis=0, keepdims=True)
    vsum[:, GAINS + D : GAINS + 2 * D] = jnp.sum(gp_ref[:, :D], axis=0, keepdims=True)
    vsum[:, GAINS + 2 * D : GAINS + 3 * D] = jnp.sum(gp_ref[:, 2 * D :], axis=0, keepdims=True)

    flat_ref[:, BIAS_ROW:, :] = jnp.zeros((BLOCKS, FIRST_ROWS - BIAS_ROW, LANES), F32)
    flat_ref[:, BIAS_ROW, :] = collect(vsum[:, GAINS:], BIAS_PART, BIASES)
    flat_ref[:, GAIN_ROW, :] = collect(vsum[:, :GAINS], GAIN_PART, GAINS)

    def pairs(p, carry):
        rows = pl.ds(pl.multiple_of(p * 2 * STRIPE, 8), 2 * STRIPE)
        for source, tiles, start in ((dwq, QKV_TILES, 0), (dwo, OUT_TILES, QKV_ROWS)):
            for t in range(tiles):
                value = source[rows, t * LANES : (t + 1) * LANES]
                for u in range(2):
                    flat_ref[2 * p + u, pl.ds(start + t, STRIPE, stride=tiles), :] = value[
                        u * STRIPE : (u + 1) * STRIPE
                    ]
        return carry

    lax.fori_loop(0, BLOCKS // 2, pairs, 0)
    pack(me, flat_ref, grads[:4], 0, 0, FIRST_HALF)
    pack(me, flat_ref, grads[4:], 1, FIRST_HALF, FIRST_HALF)


def shape(dims, kind):
    return jax.ShapeDtypeStruct(dims, kind)


def call(kernel, name, outs, scratch, cost, *operands):
    specs = [pl.BlockSpec(memory_space=pltpu.SMEM)]
    specs += [pl.BlockSpec(memory_space=pltpu.VMEM)] * (len(operands) - 1)
    return pl.pallas_call(
        kernel,
        out_shape=outs,
        in_specs=specs,
        out_specs=[pl.BlockSpec(memory_space=pltpu.VMEM)] * len(outs),
        scratch_shapes=scratch,
        compiler_params=pltpu.CompilerParams(vmem_limit_bytes=56 * 1024 * 1024),
        cost_estimate=pl.CostEstimate(flops=cost, transcendentals=0, bytes_accessed=4_000_000),
        name=name,
    )(*operands)


def attend(info, images, pieces):
    outs = [
        shape((D, 3 * D), BF16),
        shape((D, D), BF16),
        shape((1, GAINS + BIASES), F32),
        shape((ROWS, 3 * D), BF16),
        shape((ROWS, D), BF16),
    ]
    scratch = [
        pltpu.VMEM((BLOCKS, FIRST_ROWS, LANES), F32),
        pltpu.VMEM((ROWS, D), F32),
    ]
    return call(attend_kernel, "attend", outs, scratch, 5_000_000_000, info, images, *pieces)


def mlp(info, images, upstream, attended, w_out, vec, pieces):
    outs = [
        shape((IMGS, SEQ, D), BF16),
        shape((ROWS, D), F32),
        shape((1, GAINS + BIASES), F32),
    ] + [shape((8, FC_ROWS, LANES), BF16)] * 8
    scratch = [
        pltpu.VMEM((BLOCKS, FC_ROWS, LANES), F32),
        pltpu.VMEM((BLOCKS, FC_ROWS, LANES), F32),
        pltpu.VMEM((CHUNKS, D, D), BF16),
        pltpu.VMEM((CHUNKS, D, D), BF16),
        pltpu.VMEM((CHUNKS, D, D), F32),
        pltpu.VMEM((CHUNKS, D, D), F32),
        pltpu.VMEM((CHUNKS, 1, D), F32),
        pltpu.VMEM((CHUNKS, 1, D), F32),
        pltpu.VMEM((ROWS, D), F32),
        pltpu.VMEM((ROWS, D), BF16),
        pltpu.VMEM((ROWS, D), BF16),
        pltpu.VMEM((ROWS, D), F32),
        pltpu.VMEM((ROWS, D), F32),
    ]
    return call(
        mlp_kernel, "mlp", outs, scratch, 8_000_000_000,
        info, images, upstream, attended, w_out, vec, *pieces,
    )


def back(info, images, qkv, attended, grad_mid, w_qkv, w_out, vec, vec_grad):
    outs = [shape((IMGS, SEQ, D), BF16)] + [shape((8, FIRST_HALF, LANES), BF16)] * 8
    scratch = [
        pltpu.VMEM((BLOCKS, FIRST_ROWS, LANES), F32),
        pltpu.VMEM((ROWS, D), F32),
        pltpu.VMEM((ROWS, D), BF16),
        pltpu.VMEM((ROWS, 3 * D), F32),
        pltpu.VMEM((ROWS, 3 * D), BF16),
        pltpu.VMEM((D, 3 * D), F32),
        pltpu.VMEM((D, D), F32),
        pltpu.VMEM((1, GAINS + BIASES), F32),
    ]
    return call(
        back_kernel, "back", outs, scratch, 6_000_000_000,
        info, images, qkv, attended, grad_mid, w_qkv, w_out, vec, vec_grad,
    )


def exchange(value, mask):
    return lax.ppermute(value, AXES, [(i, i ^ mask) for i in range(BLOCKS)])


def gather_blocks(block):
    half = block.shape[0] // 2
    line = [block] + [exchange(block, mask) for mask in (Z_LOW, Z_HIGH, Z_LOW + Z_HIGH)]
    colors = []
    for color, (near, far) in enumerate(((Y_BIT, X_BIT), (X_BIT, Y_BIT))):
        part = slice(0, half) if color == 0 else slice(half, 2 * half)
        first = jnp.stack([piece[part] for piece in line])
        colors.append((first, exchange(first, near), far))
    pieces = []
    for first, second, far in colors:
        plane = jnp.concatenate([first, second])
        other = exchange(plane, far)
        pieces += [plane, other, exchange(plane, CORE_BIT), exchange(other, CORE_BIT)]
    return pieces


def reduce_blocks(pieces):
    done = []
    for color, (near, far) in enumerate(((Y_BIT, X_BIT), (X_BIT, Y_BIT))):
        keep, keep_far, send, send_far = pieces[4 * color : 4 * color + 4]
        far_sum = keep_far.astype(F32) + exchange(send_far, CORE_BIT).astype(F32)
        crossed = exchange(far_sum.astype(BF16), far).astype(F32)
        plane = keep.astype(F32) + exchange(send, CORE_BIT).astype(F32) + crossed
        done.append(plane[:4] + exchange(plane[4:].astype(BF16), near).astype(F32))
    line = jnp.concatenate(done, axis=1)
    total = line[0]
    for step, mask in ((1, Z_LOW), (2, Z_HIGH), (3, Z_LOW + Z_HIGH)):
        total = total + exchange(line[step].astype(BF16), mask).astype(F32)
    return total


def ordered_pieces(whole):
    half = whole.shape[1] // 2
    cube = whole.reshape(2, 2, 4, 2, 2, half, LANES)
    pieces = []
    for core in range(2):
        for far in range(2):
            pieces.append((0, core, far, cube[far, core, :, :, 0].swapaxes(0, 1)))
            pieces.append((1, core, far, cube[:, core, :, far, 1]))
    pieces.sort(key=lambda entry: entry[:3])
    return [entry[3].reshape(8, half, LANES) for entry in pieces]


def blocks_of_pieces(pieces):
    half = pieces[0].shape[1]
    first = jnp.stack(pieces[:4]).reshape(2, 2, 2, 4, half, LANES)
    second = jnp.stack(pieces[4:]).reshape(2, 2, 2, 4, half, LANES)
    first = first.transpose(1, 0, 3, 2, 4, 5)
    second = second.transpose(2, 0, 3, 1, 4, 5)
    return jnp.concatenate([first, second], axis=4).reshape(BLOCKS, 2 * half, LANES)


def block_rows(flat, rows):
    flat = flat.reshape(flat.shape[:-1] + (-1,))
    short = rows * LANES - flat.shape[-1]
    if short:
        flat = jnp.pad(flat, [(0, 0)] * (flat.ndim - 1) + [(0, short)])
    return flat.reshape(flat.shape[:-1] + (rows, LANES))


def build_first(qkv, out, gains, biases):
    tail = FIRST_ROWS - GAIN_ROW - 1
    parts = [
        block_rows(qkv, QKV_ROWS),
        block_rows(out, OUT_ROWS),
        block_rows(biases, 1),
        block_rows(gains, 1),
        jnp.zeros(qkv.shape[:-1] + (tail, LANES), qkv.dtype),
    ]
    return jnp.concatenate(parts, axis=-2)


def build_second(fc1, fc2):
    return jnp.concatenate([block_rows(fc1, FC_ROWS), block_rows(fc2, FC_ROWS)], axis=-2)


def split_first(block):
    lead = block.shape[:-2]
    return (
        block[..., :QKV_ROWS, :].reshape(lead + (-1,)),
        block[..., QKV_ROWS:BIAS_ROW, :].reshape(lead + (-1,)),
        block[..., GAIN_ROW, :GAIN_PART],
        block[..., BIAS_ROW, :BIAS_PART],
    )


def split_second(block):
    lead = block.shape[:-2]
    return (
        block[..., :FC_ROWS, :].reshape(lead + (-1,)),
        block[..., FC_ROWS:, :].reshape(lead + (-1,)),
    )


def adam_update(weight, gradient, moment_one, moment_two, step_rate, decayed):
    first_new = BETA_ONE * moment_one + (1.0 - BETA_ONE) * gradient
    second_new = BETA_TWO * moment_two + (1.0 - BETA_TWO) * gradient * gradient
    first_hat = first_new / (1.0 - BETA_ONE**ADAM_STEP)
    second_hat = second_new / (1.0 - BETA_TWO**ADAM_STEP)
    change = first_hat / (jnp.sqrt(second_hat) + ADAM_EPS)
    if decayed:
        change = change + DECAY_RATE * weight
    return (weight - step_rate * change, first_new, second_new)


def device_step(devices, images, counts, upstream, *state):
    masters, firsts, seconds = state[:6], state[6:12], state[12:18]
    index = lax.axis_index(AXES)
    live = lax.dynamic_index_in_dim(counts, index, 0, keepdims=False)
    lowered = [master.astype(BF16) for master in masters]
    swaps = devices == BLOCKS
    if swaps:
        info = jnp.stack([index, live]).astype(jnp.int32)
        first = gather_blocks(build_first(lowered[0], lowered[1], lowered[4], lowered[5]))
        second = gather_blocks(build_second(lowered[2], lowered[3]))
    else:
        info = jnp.stack([jnp.zeros_like(live), live]).astype(jnp.int32)
        whole = [
            lax.all_gather(part, AXES, axis=0, tiled=True).reshape(BLOCKS, -1) for part in lowered
        ]
        first = ordered_pieces(build_first(whole[0], whole[1], whole[4], whole[5]))
        second = ordered_pieces(build_second(whole[2], whole[3]))
    w_qkv, w_out, vec, qkv, attended = attend(info, images, first)
    block_out, grad_mid, vec_grad, *second_grads = mlp(
        info, images, upstream, attended, w_out, vec, second
    )
    images_grad, *first_grads = back(
        info, images, qkv, attended, grad_mid, w_qkv, w_out, vec, vec_grad
    )
    if swaps:
        fc1, fc2 = split_second(reduce_blocks(second_grads))
        qkv_grad, out_grad, gains, biases = split_first(reduce_blocks(first_grads))
        owned = (qkv_grad, out_grad, fc1, fc2, gains, biases)
    else:
        fc1, fc2 = split_second(blocks_of_pieces(second_grads).astype(F32))
        qkv_grad, out_grad, gains, biases = split_first(
            blocks_of_pieces(first_grads).astype(F32)
        )
        owned = tuple(
            lax.psum_scatter(part.reshape(-1), AXES, scatter_dimension=0, tiled=True)
            for part in (qkv_grad, out_grad, fc1, fc2, gains, biases)
        )
    updates = [
        adam_update(masters[p], owned[p], firsts[p], seconds[p], RATES[p], DECAYED[p])
        for p in range(6)
    ]
    return (
        block_out,
        images_grad,
        *owned,
        *(update[0] for update in updates),
        *(update[1] for update in updates),
        *(update[2] for update in updates),
    )


def solution(mesh):
    devices = math.prod(mesh.shape.values())
    slots = P(AXES, None, None)
    flat = P(AXES)

    def step(*args):
        return device_step(devices, *args)

    return jax.shard_map(
        step,
        mesh=mesh,
        in_specs=(slots, P(), slots) + (flat,) * 18,
        out_specs=(slots, slots) + (flat,) * 24,
        check_vma=False,
    )
```

```python
import functools
import math

import jax
import jax.numpy as jnp
from jax import lax
from jax.experimental import pallas as pl
from jax.experimental.pallas import tpu as pltpu
from jax.sharding import PartitionSpec as P

D = 384
HEADS = 6
HEAD_DIM = 64
FF = 1536
SEQ = 197
ADAM_STEP = 3

NORM_EPS = 1e-06
BETA_ONE = 0.9
BETA_TWO = 0.95
ADAM_EPS = 1e-08
DECAY_RATE = 0.1
RATES = (0.01, 0.05, 0.01, 0.01, 0.2, 0.2)
DECAYED = (True, True, True, True, False, False)
INV_ROOT_TWO = 0.7071067811865476
INV_ROOT_TWOPI = 0.3989422804014327

AXES = ("row", "col")
F32 = jnp.float32
BF16 = jnp.bfloat16
LANES = 128
PAD = 208
IMGS = 2
ROWS = IMGS * PAD
BLOCKS = 32
STRIPE = D // BLOCKS
QKV_TILES = 3 * D // LANES
OUT_TILES = D // LANES
FC_TILES = FF // LANES
QKV_ROWS = STRIPE * QKV_TILES
OUT_ROWS = STRIPE * OUT_TILES
FC_ROWS = STRIPE * FC_TILES
TALL = FF // BLOCKS
BIAS_ROW = QKV_ROWS
GAIN_ROW = BIAS_ROW + 1
FIRST_ROWS = 112
SECOND_SPLIT = (160, 176)
SECOND_ROWS = sum(SECOND_SPLIT)
OUT_START = FC_ROWS
FC2_START = OUT_START + OUT_ROWS
GAINS = 2 * D
BIASES = 6 * D + FF
GAIN_PART = GAINS // BLOCKS
BIAS_PART = BIASES // BLOCKS
CHUNKS = FF // D
Y_BIT, Z_LOW, Z_HIGH, CORE_BIT, X_BIT = 1, 2, 4, 8, 16


def nn(a, b):
    return jnp.dot(a, b, preferred_element_type=F32)


def nt(a, b):
    return lax.dot_general(a, b, (((1,), (1,)), ((), ())), preferred_element_type=F32)


def tn(a, b):
    return lax.dot_general(a, b, (((0,), (0,)), ((), ())), preferred_element_type=F32)


def norm_forward(row_data):
    centered = row_data - jnp.mean(row_data, axis=-1, keepdims=True)
    inv_std = lax.rsqrt(jnp.mean(centered * centered, axis=-1, keepdims=True) + NORM_EPS)
    return (centered * inv_std, inv_std)


def norm_backward(grad_hat, normed, inv_std):
    return inv_std * (
        grad_hat
        - jnp.mean(grad_hat, axis=-1, keepdims=True)
        - normed * jnp.mean(grad_hat * normed, axis=-1, keepdims=True)
    )


def masks_of(index, color):
    return (index & 3) * Z_LOW + (index >> 2) * (Y_BIT if color == 0 else X_BIT)


def variants(color):
    last = X_BIT if color == 0 else Y_BIT
    return (0, last, CORE_BIT, last + CORE_BIT)


def unpack(me, piece_refs, flat_ref, color, start, count):
    for piece_ref, extra in zip(piece_refs, variants(color)):

        def body(i, carry, piece_ref=piece_ref, extra=extra):
            owner = me ^ (masks_of(i, color) ^ extra)
            flat_ref[owner, start : start + count, :] = piece_ref[i].astype(F32)
            return carry

        lax.fori_loop(0, 8, body, 0)


def pack(me, grad_ref, out_refs, color, start, count):
    for out_ref, extra in zip(out_refs, variants(color)):

        def body(i, carry, out_ref=out_ref, extra=extra):
            owner = me ^ (masks_of(i, color) ^ extra)
            out_ref[i] = grad_ref[owner, start : start + count, :].astype(BF16)
            return carry

        lax.fori_loop(0, 8, body, 0)


def striped_rows(flat_ref, quad, start, stride):
    parts = [flat_ref[4 * quad + u, pl.ds(start, STRIPE, stride=stride), :] for u in range(4)]
    return jnp.concatenate(parts, axis=0).astype(BF16)


def scatter_rows(flat_ref, pair, start, stride, value):
    for u in range(2):
        flat_ref[2 * pair + u, pl.ds(start, STRIPE, stride=stride), :] = value[
            u * STRIPE : (u + 1) * STRIPE
        ]


def select_matrix(part, total):
    lane = lax.broadcasted_iota(jnp.int32, (LANES, total), 1)
    sub = lax.broadcasted_iota(jnp.int32, (LANES, total), 0)
    block = (lane * ((1 << 22) // part + 1)) >> 22
    return jnp.where(lane - block * part == sub, 1.0, 0.0).astype(BF16)


def owner_mask(part, total):
    lane = lax.broadcasted_iota(jnp.int32, (BLOCKS, total), 1)
    block = lax.broadcasted_iota(jnp.int32, (BLOCKS, total), 0)
    return (lane >= block * part) & (lane < block * part + part)


def spread(block_rows, part, total):
    moved = nn(block_rows.astype(BF16), select_matrix(part, total))
    return jnp.sum(jnp.where(owner_mask(part, total), moved, 0.0), axis=0, keepdims=True)


def collect(row, part, total):
    own = jnp.where(owner_mask(part, total), jnp.broadcast_to(row, (BLOCKS, total)), 0.0)
    return nt(own.astype(BF16), select_matrix(part, total))


def load_padded(x_ref, padded_ref, scales=None):
    for b in range(IMGS):
        tail = (SEQ // 16) * 16
        padded_ref[b * PAD + tail : (b + 1) * PAD, :] = jnp.zeros((PAD - tail, D), F32)
        value = x_ref[b].astype(F32)
        if scales is not None:
            value = value * scales[b]
        padded_ref[b * PAD : b * PAD + SEQ, :] = value


def bias_slice(vec_ref, start, size):
    return vec_ref[:, GAINS + start : GAINS + start + size]


def head_masks():
    lane = lax.broadcasted_iota(jnp.int32, (1, LANES), 1)
    low = jnp.where(lane < HEAD_DIM, 1.0, 0.0)
    return (low.astype(BF16), (1.0 - low).astype(BF16))


def position(swaps):
    return lax.axis_index(AXES) if swaps else jnp.int32(0)


def attend_kernel(swaps, counts_ref, x_ref, *refs):
    pieces = refs[:4]
    wqkv_ref, vec_ref, qkv_ref, att_ref = refs[4:8]
    flat_ref, pad_ref = refs[8:]
    me = position(swaps)
    unpack(me, pieces, flat_ref, 0, 0, FIRST_ROWS)

    def quads(quad, carry):
        rows = pl.ds(pl.multiple_of(quad * 4 * STRIPE, 16), 4 * STRIPE)
        for t in range(QKV_TILES):
            wqkv_ref[rows, t * LANES : (t + 1) * LANES] = striped_rows(
                flat_ref, quad, t, QKV_TILES
            )
        return carry

    lax.fori_loop(0, BLOCKS // 4, quads, 0)
    vec_ref[:, :GAINS] = spread(flat_ref[:, GAIN_ROW, :], GAIN_PART, GAINS)
    vec_ref[:, GAINS:] = spread(flat_ref[:, BIAS_ROW, :], BIAS_PART, BIASES)

    load_padded(x_ref, pad_ref)
    hat_in, _ = norm_forward(pad_ref[...])
    normed_in = (hat_in * vec_ref[:, :D] + bias_slice(vec_ref, 0, D)).astype(BF16)
    qkv_ref[:, :D] = (
        nn(normed_in, wqkv_ref[:, :D]) + bias_slice(vec_ref, D, D)
    ).astype(BF16)
    qkv_ref[:, D : 2 * D] = nn(normed_in, wqkv_ref[:, D : 2 * D]).astype(BF16)
    qkv_ref[:, 2 * D :] = (
        nn(normed_in, wqkv_ref[:, 2 * D :]) + bias_slice(vec_ref, 2 * D, D)
    ).astype(BF16)

    masks = head_masks()
    lane = lax.broadcasted_iota(jnp.int32, (1, LANES), 1)
    dead = jnp.where(lax.broadcasted_iota(jnp.int32, (1, PAD), 1) < SEQ, 0.0, -1e30)

    def image(b, carry):
        rows = pl.ds(pl.multiple_of(b * PAD, 16), PAD)
        for pair in range(HEADS // 2):
            cols = pair * LANES
            q2 = qkv_ref[rows, cols : cols + LANES]
            k2 = qkv_ref[rows, D + cols : D + cols + LANES]
            v2 = qkv_ref[rows, 2 * D + cols : 2 * D + cols + LANES]
            outs = []
            for mask in masks:
                scores = nt(q2 * mask, k2) * HEAD_DIM ** (-0.5) + dead
                top = jnp.max(scores, axis=-1, keepdims=True)
                grown = jnp.exp(scores - top)
                total = jnp.sum(grown, axis=-1, keepdims=True)
                probs = (grown * (1.0 / total)).astype(BF16)
                outs.append(nn(probs, v2))
            att_ref[rows, cols : cols + LANES] = jnp.where(
                lane < HEAD_DIM, outs[0], outs[1]
            ).astype(BF16)
        return carry

    lax.fori_loop(0, IMGS, image, 0)


def mlp_kernel(swaps, counts_ref, x_ref, up_ref, att_ref, vec_ref, *refs):
    pieces = refs[:8]
    out_ref, gmid_ref, vecg_ref, wout_ref = refs[8:12]
    grads = refs[12:20]
    flat_ref, w1, w2, dw1, dw2, dwo, b1, b1g, pad_ref, go_ref, nm_ref, acc, gacc = refs[20:]
    me = position(swaps)
    count = counts_ref[lax.axis_index(AXES)]
    live = [jnp.where(count > b, 1.0, 0.0).astype(F32) for b in range(IMGS)]
    unpack(me, pieces[:4], flat_ref, 0, 0, SECOND_SPLIT[0])
    unpack(me, pieces[4:], flat_ref, 1, *SECOND_SPLIT)

    def quads(quad, carry):
        rows = pl.ds(pl.multiple_of(quad * 4 * STRIPE, 16), 4 * STRIPE)
        for t in range(FC_TILES):
            w1[t // 3, rows, (t % 3) * LANES : (t % 3 + 1) * LANES] = striped_rows(
                flat_ref, quad, t, FC_TILES
            )
        for t in range(OUT_TILES):
            wout_ref[rows, t * LANES : (t + 1) * LANES] = striped_rows(
                flat_ref, quad, OUT_START + t, OUT_TILES
            )
        return carry

    lax.fori_loop(0, BLOCKS // 4, quads, 0)

    def talls(d, carry):
        rows = pl.ds(pl.multiple_of((d & 7) * TALL, 16), TALL)
        for t in range(OUT_TILES):
            w2[d >> 3, rows, t * LANES : (t + 1) * LANES] = flat_ref[
                d, pl.ds(FC2_START + t, TALL, stride=OUT_TILES), :
            ].astype(BF16)
        return carry

    lax.fori_loop(0, BLOCKS, talls, 0)
    for j in range(CHUNKS):
        b1[j] = bias_slice(vec_ref, 5 * D + j * D, D)

    load_padded(x_ref, pad_ref)
    load_padded(up_ref, acc, live)
    go_ref[...] = acc[...].astype(BF16)
    mid = pad_ref[...] + nn(att_ref[...], wout_ref[...]) + bias_slice(vec_ref, 3 * D, D)
    hat_mid, inv_mid = norm_forward(mid)
    nm_ref[...] = (hat_mid * vec_ref[:, D : 2 * D] + bias_slice(vec_ref, 4 * D, D)).astype(BF16)
    acc[...] = mid + bias_slice(vec_ref, 5 * D + FF, D)
    pad_ref[...] = mid
    gacc[...] = jnp.zeros((ROWS, D), F32)

    def chunk(j, carry):
        hidden = nn(nm_ref[...], w1[j]) + b1[j]
        cdf = 0.5 * (1.0 + lax.erf(hidden * INV_ROOT_TWO))
        act = (hidden * cdf).astype(BF16)
        slope = cdf + hidden * INV_ROOT_TWOPI * jnp.exp(-0.5 * hidden * hidden)
        acc[...] += nn(act, w2[j])
        dw2[j] = tn(act, go_ref[...])
        grad_pre = nt(go_ref[...], w2[j]) * slope
        b1g[j] = jnp.sum(grad_pre, axis=0, keepdims=True)
        grad_pre_bf = grad_pre.astype(BF16)
        dw1[j] = tn(nm_ref[...], grad_pre_bf)
        gacc[...] += nt(grad_pre_bf, w1[j])
        return carry

    lax.fori_loop(0, CHUNKS, chunk, 0)
    for b in range(IMGS):
        out_ref[b] = (acc[b * PAD : b * PAD + SEQ, :] * live[b]).astype(BF16)

    hat_mid, inv_mid = norm_forward(pad_ref[...])
    grad_normed = gacc[...]
    grad_float = go_ref[...].astype(F32)
    grad_mid = grad_float + norm_backward(grad_normed * vec_ref[:, D : 2 * D], hat_mid, inv_mid)
    gmid_ref[...] = grad_mid
    dwo[...] = tn(att_ref[...], grad_mid.astype(BF16))
    vecg_ref[...] = jnp.zeros((1, GAINS + BIASES), F32)
    vecg_ref[:, D : 2 * D] = jnp.sum(grad_normed * hat_mid, axis=0, keepdims=True)
    base = GAINS
    vecg_ref[:, base + 3 * D : base + 4 * D] = jnp.sum(grad_mid, axis=0, keepdims=True)
    vecg_ref[:, base + 4 * D : base + 5 * D] = jnp.sum(grad_normed, axis=0, keepdims=True)
    for j in range(CHUNKS):
        vecg_ref[:, base + (5 + j) * D : base + (6 + j) * D] = b1g[j]
    vecg_ref[:, base + 5 * D + FF :] = jnp.sum(grad_float, axis=0, keepdims=True)

    def pairs(p, carry):
        rows = pl.ds(pl.multiple_of(p * 2 * STRIPE, 8), 2 * STRIPE)
        for t in range(FC_TILES):
            value = dw1[t // 3, rows, (t % 3) * LANES : (t % 3 + 1) * LANES]
            scatter_rows(flat_ref, p, t, FC_TILES, value)
        for t in range(OUT_TILES):
            scatter_rows(
                flat_ref, p, OUT_START + t, OUT_TILES, dwo[rows, t * LANES : (t + 1) * LANES]
            )
        return carry

    lax.fori_loop(0, BLOCKS // 2, pairs, 0)

    def talls_back(d, carry):
        rows = pl.ds(pl.multiple_of((d & 7) * TALL, 16), TALL)
        for t in range(OUT_TILES):
            flat_ref[d, pl.ds(FC2_START + t, TALL, stride=OUT_TILES), :] = dw2[
                d >> 3, rows, t * LANES : (t + 1) * LANES
            ]
        return carry

    lax.fori_loop(0, BLOCKS, talls_back, 0)
    used = FC2_START + FC_ROWS
    flat_ref[:, used:, :] = jnp.zeros((BLOCKS, SECOND_ROWS - used, LANES), F32)
    pack(me, flat_ref, grads[:4], 0, 0, SECOND_SPLIT[0])
    pack(me, flat_ref, grads[4:], 1, *SECOND_SPLIT)


def back_kernel(
    swaps, counts_ref, x_ref, qkv_ref, gmid_ref, wqkv_ref, wout_ref, vec_ref, vecg_ref, *refs
):
    xgrad_ref = refs[0]
    grads = refs[1:5]
    flat_ref, pad_ref, ga_ref, gp_ref, gpb_ref, dwq, vsum = refs[5:]
    me = position(swaps)
    gmid_bf = gmid_ref[...].astype(BF16)
    ga_ref[...] = nt(gmid_bf, wout_ref[...]).astype(BF16)

    masks = head_masks()
    alive = jnp.where(lax.broadcasted_iota(jnp.int32, (PAD, 1), 0) < SEQ, 0.0, -1e30)

    def image(b, carry):
        rows = pl.ds(pl.multiple_of(b * PAD, 16), PAD)
        for pair in range(HEADS // 2):
            cols = pair * LANES
            q2 = qkv_ref[rows, cols : cols + LANES]
            k2 = qkv_ref[rows, D + cols : D + cols + LANES]
            v2 = qkv_ref[rows, 2 * D + cols : 2 * D + cols + LANES]
            g2 = ga_ref[rows, cols : cols + LANES]
            gq = jnp.zeros((PAD, LANES), F32)
            gk = jnp.zeros((PAD, LANES), F32)
            gv = jnp.zeros((PAD, LANES), F32)
            for mask in masks:
                qm = q2 * mask
                gm = g2 * mask
                scores = nt(k2, qm) * HEAD_DIM ** (-0.5) + alive
                top = jnp.max(scores, axis=0, keepdims=True)
                grown = jnp.exp(scores - top)
                total = jnp.sum(grown, axis=0, keepdims=True)
                probs = grown * (1.0 / total)
                grad_probs = nt(v2, gm)
                row_dot = jnp.sum(probs * grad_probs, axis=0, keepdims=True)
                grad_scores = (probs * (grad_probs - row_dot) * HEAD_DIM ** (-0.5)).astype(BF16)
                gv = gv + nn(probs.astype(BF16), gm)
                gk = gk + nn(grad_scores, qm)
                gq = gq + tn(grad_scores, k2 * mask)
            gp_ref[rows, cols : cols + LANES] = gq
            gp_ref[rows, D + cols : D + cols + LANES] = gk
            gp_ref[rows, 2 * D + cols : 2 * D + cols + LANES] = gv
        return carry

    lax.fori_loop(0, IMGS, image, 0)

    load_padded(x_ref, pad_ref)
    hat_in, inv_in = norm_forward(pad_ref[...])
    normed_in = (hat_in * vec_ref[:, :D] + bias_slice(vec_ref, 0, D)).astype(BF16)
    gpb_ref[...] = gp_ref[...].astype(BF16)
    dwq[...] = tn(normed_in, gpb_ref[...])
    grad_in = nt(gpb_ref[...], wqkv_ref[...])
    images_grad = gmid_ref[...] + norm_backward(grad_in * vec_ref[:, :D], hat_in, inv_in)
    pad_ref[...] = images_grad
    for b in range(IMGS):
        xgrad_ref[b] = pad_ref[b * PAD : b * PAD + SEQ, :].astype(BF16)

    vsum[...] = vecg_ref[...]
    vsum[:, :D] = jnp.sum(grad_in * hat_in, axis=0, keepdims=True)
    vsum[:, GAINS : GAINS + D] = jnp.sum(grad_in, axis=0, keepdims=True)
    vsum[:, GAINS + D : GAINS + 2 * D] = jnp.sum(gp_ref[:, :D], axis=0, keepdims=True)
    vsum[:, GAINS + 2 * D : GAINS + 3 * D] = jnp.sum(gp_ref[:, 2 * D :], axis=0, keepdims=True)

    flat_ref[:, BIAS_ROW:, :] = jnp.zeros((BLOCKS, FIRST_ROWS - BIAS_ROW, LANES), F32)
    flat_ref[:, BIAS_ROW, :] = collect(vsum[:, GAINS:], BIAS_PART, BIASES)
    flat_ref[:, GAIN_ROW, :] = collect(vsum[:, :GAINS], GAIN_PART, GAINS)

    def pairs(p, carry):
        rows = pl.ds(pl.multiple_of(p * 2 * STRIPE, 8), 2 * STRIPE)
        for t in range(QKV_TILES):
            scatter_rows(flat_ref, p, t, QKV_TILES, dwq[rows, t * LANES : (t + 1) * LANES])
        return carry

    lax.fori_loop(0, BLOCKS // 2, pairs, 0)
    pack(me, flat_ref, grads, 0, 0, FIRST_ROWS)


def shape(dims, kind):
    return jax.ShapeDtypeStruct(dims, kind)


def call(kernel, swaps, outs, scratch, cost, *operands):
    specs = [pl.BlockSpec(memory_space=pltpu.SMEM)]
    specs += [pl.BlockSpec(memory_space=pltpu.VMEM)] * (len(operands) - 1)
    return pl.pallas_call(
        functools.partial(kernel, swaps),
        out_shape=outs,
        in_specs=specs,
        out_specs=[pl.BlockSpec(memory_space=pltpu.VMEM)] * len(outs),
        scratch_shapes=scratch,
        compiler_params=pltpu.CompilerParams(vmem_limit_bytes=56 * 1024 * 1024),
        cost_estimate=pl.CostEstimate(flops=cost, transcendentals=0, bytes_accessed=4_000_000),
    )(*operands)


def attend(swaps, counts, images, pieces):
    outs = [
        shape((D, 3 * D), BF16),
        shape((1, GAINS + BIASES), F32),
        shape((ROWS, 3 * D), BF16),
        shape((ROWS, D), BF16),
    ]
    scratch = [
        pltpu.VMEM((BLOCKS, FIRST_ROWS, LANES), F32),
        pltpu.VMEM((ROWS, D), F32),
    ]
    return call(attend_kernel, swaps, outs, scratch, 5_000_000_000, counts, images, *pieces)


def piece_shapes(*split):
    return [shape((8, rows, LANES), BF16) for rows in split for _ in range(4)]


def mlp(swaps, counts, images, upstream, attended, vec, pieces):
    outs = [
        shape((IMGS, SEQ, D), BF16),
        shape((ROWS, D), F32),
        shape((1, GAINS + BIASES), F32),
        shape((D, D), BF16),
    ] + piece_shapes(*SECOND_SPLIT)
    scratch = [
        pltpu.VMEM((BLOCKS, SECOND_ROWS, LANES), F32),
        pltpu.VMEM((CHUNKS, D, D), BF16),
        pltpu.VMEM((CHUNKS, D, D), BF16),
        pltpu.VMEM((CHUNKS, D, D), F32),
        pltpu.VMEM((CHUNKS, D, D), F32),
        pltpu.VMEM((D, D), F32),
        pltpu.VMEM((CHUNKS, 1, D), F32),
        pltpu.VMEM((CHUNKS, 1, D), F32),
        pltpu.VMEM((ROWS, D), F32),
        pltpu.VMEM((ROWS, D), BF16),
        pltpu.VMEM((ROWS, D), BF16),
        pltpu.VMEM((ROWS, D), F32),
        pltpu.VMEM((ROWS, D), F32),
    ]
    return call(
        mlp_kernel, swaps, outs, scratch, 8_000_000_000,
        counts, images, upstream, attended, vec, *pieces,
    )


def back(swaps, counts, images, qkv, grad_mid, w_qkv, w_out, vec, vec_grad):
    outs = [shape((IMGS, SEQ, D), BF16)] + piece_shapes(FIRST_ROWS)
    scratch = [
        pltpu.VMEM((BLOCKS, FIRST_ROWS, LANES), F32),
        pltpu.VMEM((ROWS, D), F32),
        pltpu.VMEM((ROWS, D), BF16),
        pltpu.VMEM((ROWS, 3 * D), F32),
        pltpu.VMEM((ROWS, 3 * D), BF16),
        pltpu.VMEM((D, 3 * D), F32),
        pltpu.VMEM((1, GAINS + BIASES), F32),
    ]
    return call(
        back_kernel, swaps, outs, scratch, 6_000_000_000,
        counts, images, qkv, grad_mid, w_qkv, w_out, vec, vec_grad,
    )


def exchange(value, mask):
    return lax.ppermute(value, AXES, [(i, i ^ mask) for i in range(BLOCKS)])


def gather_line(block):
    held = block[None]
    for mask in (Z_LOW, Z_HIGH, Y_BIT):
        held = jnp.concatenate([held, exchange(held, mask)])
    other = exchange(held, X_BIT)
    core = exchange(held, CORE_BIT)
    last = exchange(other, CORE_BIT)
    return [held, other, core, last]


def reduce_line(pieces):
    keep, keep_far, send, send_far = pieces
    from_core = exchange(send_far, CORE_BIT)
    far_sum = keep_far.astype(F32) + from_core.astype(F32)
    crossed = exchange(far_sum.astype(BF16), X_BIT)
    from_core = exchange(send, CORE_BIT)
    held = keep.astype(F32) + from_core.astype(F32) + crossed.astype(F32)
    for mask in (Y_BIT, Z_HIGH, Z_LOW):
        half = held.shape[0] // 2
        crossed = exchange(held[half:].astype(BF16), mask)
        held = held[:half] + crossed.astype(F32)
    return held[0]


def gather_blocks(block, split):
    line = [block]
    for mask in (Z_LOW, Z_HIGH, Z_LOW + Z_HIGH):
        line.append(exchange(block, mask))
    colors = []
    for color, (near, far) in enumerate(((Y_BIT, X_BIT), (X_BIT, Y_BIT))):
        part = slice(0, split[0]) if color == 0 else slice(split[0], None)
        first = jnp.stack([piece[part] for piece in line])
        colors.append((first, exchange(first, near), far))
    pieces = []
    for first, second, far in colors:
        plane = jnp.concatenate([first, second])
        other = exchange(plane, far)
        core = exchange(plane, CORE_BIT)
        last = exchange(other, CORE_BIT)
        pieces += [plane, other, core, last]
    return pieces


def reduce_blocks(pieces):
    done = []
    for color, (near, far) in enumerate(((Y_BIT, X_BIT), (X_BIT, Y_BIT))):
        keep, keep_far, send, send_far = pieces[4 * color : 4 * color + 4]
        from_core = exchange(send_far, CORE_BIT)
        far_sum = keep_far.astype(F32) + from_core.astype(F32)
        crossed = exchange(far_sum.astype(BF16), far)
        from_core = exchange(send, CORE_BIT)
        plane = keep.astype(F32) + from_core.astype(F32) + crossed.astype(F32)
        crossed = exchange(plane[4:].astype(BF16), near)
        done.append(plane[:4] + crossed.astype(F32))
    line = jnp.concatenate(done, axis=1)
    total = line[0]
    for step, mask in ((1, Z_LOW), (2, Z_HIGH), (3, Z_LOW + Z_HIGH)):
        crossed = exchange(line[step].astype(BF16), mask)
        total = total + crossed.astype(F32)
    return total


def ordered_pieces(whole, split):
    cube = whole.reshape(2, 2, 4, 2, -1, LANES)
    if len(split) == 1:
        pieces = [cube[x, core].swapaxes(0, 1) for core in range(2) for x in range(2)]
        return [piece.reshape((8,) + piece.shape[2:]) for piece in pieces]
    near, far = cube[..., : split[0], :], cube[..., split[0] :, :]
    pieces = [near[x, core].swapaxes(0, 1) for core in range(2) for x in range(2)]
    pieces += [far[:, core, :, y] for core in range(2) for y in range(2)]
    return [piece.reshape((8,) + piece.shape[2:]) for piece in pieces]


def blocks_of_pieces(pieces):
    first = jnp.stack(pieces[:4]).reshape(2, 2, 2, 4, -1, LANES)
    if len(pieces) == 4:
        return first.transpose(1, 0, 3, 2, 4, 5).reshape(BLOCKS, -1, LANES)
    second = jnp.stack(pieces[4:]).reshape(2, 2, 2, 4, -1, LANES)
    first = first.transpose(1, 0, 3, 2, 4, 5)
    second = second.transpose(2, 0, 3, 1, 4, 5)
    return jnp.concatenate([first, second], axis=4).reshape(BLOCKS, -1, LANES)


def block_rows(flat, rows):
    flat = flat.reshape(flat.shape[:-1] + (-1,))
    short = rows * LANES - flat.shape[-1]
    if short:
        flat = jnp.pad(flat, [(0, 0)] * (flat.ndim - 1) + [(0, short)])
    return flat.reshape(flat.shape[:-1] + (rows, LANES))


def padded_rows(parts, rows):
    short = rows - sum(part.shape[-2] for part in parts)
    filler = jnp.zeros(parts[0].shape[:-2] + (short, LANES), parts[0].dtype)
    return jnp.concatenate([*parts, filler], axis=-2)


def build_first(qkv, gains, biases):
    parts = [block_rows(qkv, QKV_ROWS), block_rows(biases, 1), block_rows(gains, 1)]
    return padded_rows(parts, FIRST_ROWS)


def build_second(out, fc1, fc2):
    parts = [block_rows(fc1, FC_ROWS), block_rows(out, OUT_ROWS), block_rows(fc2, FC_ROWS)]
    return padded_rows(parts, SECOND_ROWS)


def flat_rows(block, start, rows):
    return block[..., start : start + rows, :].reshape(block.shape[:-2] + (-1,))


def split_blocks(first, second):
    return (
        flat_rows(first, 0, QKV_ROWS),
        flat_rows(second, OUT_START, OUT_ROWS),
        flat_rows(second, 0, FC_ROWS),
        flat_rows(second, FC2_START, FC_ROWS),
        first[..., GAIN_ROW, :GAIN_PART],
        first[..., BIAS_ROW, :BIAS_PART],
    )


def adam_update(weight, gradient, moment_one, moment_two, step_rate, decayed):
    first_new = BETA_ONE * moment_one + (1.0 - BETA_ONE) * gradient
    second_new = BETA_TWO * moment_two + (1.0 - BETA_TWO) * gradient * gradient
    first_hat = first_new / (1.0 - BETA_ONE**ADAM_STEP)
    second_hat = second_new / (1.0 - BETA_TWO**ADAM_STEP)
    change = first_hat / (jnp.sqrt(second_hat) + ADAM_EPS)
    if decayed:
        change = change + DECAY_RATE * weight
    return (weight - step_rate * change, first_new, second_new)


def device_step(devices, images, counts, upstream, *state):
    masters, firsts, seconds = state[:6], state[6:12], state[12:18]
    lowered = [master.astype(BF16) for master in masters]
    swaps = devices == BLOCKS
    if swaps:
        qkv, out, fc1, fc2, gains, biases = lowered
        first = gather_line(build_first(qkv, gains, biases))
        second = gather_blocks(build_second(out, fc1, fc2), SECOND_SPLIT)
    else:
        qkv, out, fc1, fc2, gains, biases = [
            lax.all_gather(part, AXES, axis=0, tiled=True).reshape(BLOCKS, -1) for part in lowered
        ]
        first = ordered_pieces(build_first(qkv, gains, biases), (FIRST_ROWS,))
        second = ordered_pieces(build_second(out, fc1, fc2), SECOND_SPLIT)
    w_qkv, vec, qkv, attended = attend(swaps, counts, images, first)
    block_out, grad_mid, vec_grad, w_out, *second_grads = mlp(
        swaps, counts, images, upstream, attended, vec, second
    )
    images_grad, *first_grads = back(
        swaps, counts, images, qkv, grad_mid, w_qkv, w_out, vec, vec_grad
    )
    if swaps:
        second_sum = reduce_blocks(second_grads)
        first_sum = reduce_line(first_grads)
        owned = split_blocks(first_sum, second_sum)
    else:
        owned = tuple(
            lax.psum_scatter(part.reshape(-1), AXES, scatter_dimension=0, tiled=True)
            for part in split_blocks(
                blocks_of_pieces(first_grads).astype(F32),
                blocks_of_pieces(second_grads).astype(F32),
            )
        )
    updates = [
        adam_update(masters[p], owned[p], firsts[p], seconds[p], RATES[p], DECAYED[p])
        for p in range(6)
    ]
    return (
        block_out,
        images_grad,
        *owned,
        *(update[0] for update in updates),
        *(update[1] for update in updates),
        *(update[2] for update in updates),
    )


def solution(mesh):
    devices = math.prod(mesh.shape.values())
    slots = P(AXES, None, None)
    flat = P(AXES)

    def step(*args):
        return device_step(devices, *args)

    return jax.shard_map(
        step,
        mesh=mesh,
        in_specs=(slots, P(), slots) + (flat,) * 18,
        out_specs=(slots, slots) + (flat,) * 24,
        check_vma=False,
    )
```

```python
import functools
import math

import jax
import jax.numpy as jnp
from jax import lax
from jax.experimental import pallas as pl
from jax.experimental.pallas import tpu as pltpu
from jax.sharding import PartitionSpec as P

D = 384
HEADS = 6
HEAD_DIM = 64
FF = 1536
SEQ = 197
ADAM_STEP = 3

NORM_EPS = 1e-06
BETA_ONE = 0.9
BETA_TWO = 0.95
ADAM_EPS = 1e-08
DECAY_RATE = 0.1
RATES = (0.01, 0.05, 0.01, 0.01, 0.2, 0.2)
DECAYED = (True, True, True, True, False, False)
INV_ROOT_TWO = 0.7071067811865476
INV_ROOT_TWOPI = 0.3989422804014327

AXES = ("row", "col")
F32 = jnp.float32
BF16 = jnp.bfloat16
LANES = 128
PAD = 208
IMGS = 2
ROWS = IMGS * PAD
BLOCKS = 32
STRIPE = D // BLOCKS
QKV_TILES = 3 * D // LANES
OUT_TILES = D // LANES
FC_TILES = FF // LANES
QKV_ROWS = STRIPE * QKV_TILES
OUT_ROWS = STRIPE * OUT_TILES
FC_ROWS = STRIPE * FC_TILES
TALL = FF // BLOCKS
BIAS_ROW = QKV_ROWS
GAIN_ROW = BIAS_ROW + 1
FIRST_ROWS = 112
SECOND_SPLIT = (160, 176)
SECOND_ROWS = sum(SECOND_SPLIT)
OUT_START = FC_ROWS
FC2_START = OUT_START + OUT_ROWS
GAINS = 2 * D
BIASES = 6 * D + FF
GAIN_PART = GAINS // BLOCKS
BIAS_PART = BIASES // BLOCKS
CHUNKS = FF // D
Y_BIT, Z_LOW, Z_HIGH, CORE_BIT, X_BIT = 1, 2, 4, 8, 16


def nn(a, b):
    return jnp.dot(a, b, preferred_element_type=F32)


def nt(a, b):
    return lax.dot_general(a, b, (((1,), (1,)), ((), ())), preferred_element_type=F32)


def tn(a, b):
    return lax.dot_general(a, b, (((0,), (0,)), ((), ())), preferred_element_type=F32)


def norm_forward(row_data):
    centered = row_data - jnp.mean(row_data, axis=-1, keepdims=True)
    inv_std = lax.rsqrt(jnp.mean(centered * centered, axis=-1, keepdims=True) + NORM_EPS)
    return (centered * inv_std, inv_std)


def norm_backward(grad_hat, normed, inv_std):
    return inv_std * (
        grad_hat
        - jnp.mean(grad_hat, axis=-1, keepdims=True)
        - normed * jnp.mean(grad_hat * normed, axis=-1, keepdims=True)
    )


def masks_of(index, color):
    return (index & 3) * Z_LOW + (index >> 2) * (Y_BIT if color == 0 else X_BIT)


def variants(color):
    last = X_BIT if color == 0 else Y_BIT
    return (0, last, CORE_BIT, last + CORE_BIT)


def unpack(me, piece_refs, flat_ref, color, start, count):
    for piece_ref, extra in zip(piece_refs, variants(color)):

        def body(i, carry, piece_ref=piece_ref, extra=extra):
            owner = me ^ (masks_of(i, color) ^ extra)
            flat_ref[owner, start : start + count, :] = piece_ref[i].astype(F32)
            return carry

        lax.fori_loop(0, 8, body, 0)


def pack(me, grad_ref, out_refs, color, start, count):
    for out_ref, extra in zip(out_refs, variants(color)):

        def body(i, carry, out_ref=out_ref, extra=extra):
            owner = me ^ (masks_of(i, color) ^ extra)
            out_ref[i] = grad_ref[owner, start : start + count, :].astype(BF16)
            return carry

        lax.fori_loop(0, 8, body, 0)


def striped_rows(flat_ref, quad, start, stride):
    parts = [flat_ref[4 * quad + u, pl.ds(start, STRIPE, stride=stride), :] for u in range(4)]
    return jnp.concatenate(parts, axis=0).astype(BF16)


def scatter_rows(flat_ref, pair, start, stride, value):
    for u in range(2):
        flat_ref[2 * pair + u, pl.ds(start, STRIPE, stride=stride), :] = value[
            u * STRIPE : (u + 1) * STRIPE
        ]


def select_matrix(part, total):
    lane = lax.broadcasted_iota(jnp.int32, (LANES, total), 1)
    sub = lax.broadcasted_iota(jnp.int32, (LANES, total), 0)
    block = (lane * ((1 << 22) // part + 1)) >> 22
    return jnp.where(lane - block * part == sub, 1.0, 0.0).astype(BF16)


def owner_mask(part, total):
    lane = lax.broadcasted_iota(jnp.int32, (BLOCKS, total), 1)
    block = lax.broadcasted_iota(jnp.int32, (BLOCKS, total), 0)
    return (lane >= block * part) & (lane < block * part + part)


def spread(block_rows, part, total):
    moved = nn(block_rows.astype(BF16), select_matrix(part, total))
    return jnp.sum(jnp.where(owner_mask(part, total), moved, 0.0), axis=0, keepdims=True)


def collect(row, part, total):
    own = jnp.where(owner_mask(part, total), jnp.broadcast_to(row, (BLOCKS, total)), 0.0)
    return nt(own.astype(BF16), select_matrix(part, total))


def load_padded(x_ref, padded_ref, scales=None):
    for b in range(IMGS):
        tail = (SEQ // 16) * 16
        padded_ref[b * PAD + tail : (b + 1) * PAD, :] = jnp.zeros((PAD - tail, D), F32)
        value = x_ref[b].astype(F32)
        if scales is not None:
            value = value * scales[b]
        padded_ref[b * PAD : b * PAD + SEQ, :] = value


def bias_slice(vec_ref, start, size):
    return vec_ref[:, GAINS + start : GAINS + start + size]


def head_masks():
    lane = lax.broadcasted_iota(jnp.int32, (1, LANES), 1)
    low = jnp.where(lane < HEAD_DIM, 1.0, 0.0)
    return (low.astype(BF16), (1.0 - low).astype(BF16))


def position(swaps):
    return lax.axis_index(AXES) if swaps else jnp.int32(0)


def attend_kernel(swaps, counts_ref, x_ref, *refs):
    pieces = refs[:4]
    wqkv_ref, vec_ref, qkv_ref, att_ref = refs[4:8]
    flat_ref, pad_ref = refs[8:]
    me = position(swaps)
    unpack(me, pieces, flat_ref, 0, 0, FIRST_ROWS)

    def quads(quad, carry):
        rows = pl.ds(pl.multiple_of(quad * 4 * STRIPE, 16), 4 * STRIPE)
        for t in range(QKV_TILES):
            wqkv_ref[rows, t * LANES : (t + 1) * LANES] = striped_rows(
                flat_ref, quad, t, QKV_TILES
            )
        return carry

    lax.fori_loop(0, BLOCKS // 4, quads, 0)
    vec_ref[:, :GAINS] = spread(flat_ref[:, GAIN_ROW, :], GAIN_PART, GAINS)
    vec_ref[:, GAINS:] = spread(flat_ref[:, BIAS_ROW, :], BIAS_PART, BIASES)

    load_padded(x_ref, pad_ref)
    hat_in, _ = norm_forward(pad_ref[...])
    normed_in = (hat_in * vec_ref[:, :D] + bias_slice(vec_ref, 0, D)).astype(BF16)
    qkv_ref[:, :D] = (
        nn(normed_in, wqkv_ref[:, :D]) + bias_slice(vec_ref, D, D)
    ).astype(BF16)
    qkv_ref[:, D : 2 * D] = nn(normed_in, wqkv_ref[:, D : 2 * D]).astype(BF16)
    qkv_ref[:, 2 * D :] = (
        nn(normed_in, wqkv_ref[:, 2 * D :]) + bias_slice(vec_ref, 2 * D, D)
    ).astype(BF16)

    masks = head_masks()
    lane = lax.broadcasted_iota(jnp.int32, (1, LANES), 1)
    dead = jnp.where(lax.broadcasted_iota(jnp.int32, (1, PAD), 1) < SEQ, 0.0, -1e30)

    def image(b, carry):
        rows = pl.ds(pl.multiple_of(b * PAD, 16), PAD)
        for pair in range(HEADS // 2):
            cols = pair * LANES
            q2 = qkv_ref[rows, cols : cols + LANES]
            k2 = qkv_ref[rows, D + cols : D + cols + LANES]
            v2 = qkv_ref[rows, 2 * D + cols : 2 * D + cols + LANES]
            outs = []
            for mask in masks:
                scores = nt(q2 * mask, k2) * HEAD_DIM ** (-0.5) + dead
                top = jnp.max(scores, axis=-1, keepdims=True)
                grown = jnp.exp(scores - top)
                total = jnp.sum(grown, axis=-1, keepdims=True)
                probs = (grown * (1.0 / total)).astype(BF16)
                outs.append(nn(probs, v2))
            att_ref[rows, cols : cols + LANES] = jnp.where(
                lane < HEAD_DIM, outs[0], outs[1]
            ).astype(BF16)
        return carry

    lax.fori_loop(0, IMGS, image, 0)


def mlp_kernel(swaps, counts_ref, x_ref, up_ref, att_ref, vec_ref, *refs):
    pieces = refs[:8]
    out_ref, gmid_ref, vecg_ref, wout_ref = refs[8:12]
    grads = refs[12:20]
    flat_ref, w1, w2, dw1, dw2, dwo, b1, b1g, pad_ref, go_ref, nm_ref, acc, gacc = refs[20:]
    me = position(swaps)
    count = counts_ref[lax.axis_index(AXES)]
    live = [jnp.where(count > b, 1.0, 0.0).astype(F32) for b in range(IMGS)]
    unpack(me, pieces[:4], flat_ref, 0, 0, SECOND_SPLIT[0])
    unpack(me, pieces[4:], flat_ref, 1, *SECOND_SPLIT)

    def quads(quad, carry):
        rows = pl.ds(pl.multiple_of(quad * 4 * STRIPE, 16), 4 * STRIPE)
        for t in range(FC_TILES):
            w1[t // 3, rows, (t % 3) * LANES : (t % 3 + 1) * LANES] = striped_rows(
                flat_ref, quad, t, FC_TILES
            )
        for t in range(OUT_TILES):
            wout_ref[rows, t * LANES : (t + 1) * LANES] = striped_rows(
                flat_ref, quad, OUT_START + t, OUT_TILES
            )
        return carry

    lax.fori_loop(0, BLOCKS // 4, quads, 0)

    def talls(d, carry):
        rows = pl.ds(pl.multiple_of((d & 7) * TALL, 16), TALL)
        for t in range(OUT_TILES):
            w2[d >> 3, rows, t * LANES : (t + 1) * LANES] = flat_ref[
                d, pl.ds(FC2_START + t, TALL, stride=OUT_TILES), :
            ].astype(BF16)
        return carry

    lax.fori_loop(0, BLOCKS, talls, 0)
    for j in range(CHUNKS):
        b1[j] = bias_slice(vec_ref, 5 * D + j * D, D)

    load_padded(x_ref, pad_ref)
    load_padded(up_ref, acc, live)
    go_ref[...] = acc[...].astype(BF16)
    mid = pad_ref[...] + nn(att_ref[...], wout_ref[...]) + bias_slice(vec_ref, 3 * D, D)
    hat_mid, inv_mid = norm_forward(mid)
    nm_ref[...] = (hat_mid * vec_ref[:, D : 2 * D] + bias_slice(vec_ref, 4 * D, D)).astype(BF16)
    acc[...] = mid + bias_slice(vec_ref, 5 * D + FF, D)
    pad_ref[...] = mid
    gacc[...] = jnp.zeros((ROWS, D), F32)

    def chunk(j, carry):
        hidden = nn(nm_ref[...], w1[j]) + b1[j]
        cdf = 0.5 * (1.0 + lax.erf(hidden * INV_ROOT_TWO))
        act = (hidden * cdf).astype(BF16)
        slope = cdf + hidden * INV_ROOT_TWOPI * jnp.exp(-0.5 * hidden * hidden)
        acc[...] += nn(act, w2[j])
        dw2[j] = tn(act, go_ref[...])
        grad_pre = nt(go_ref[...], w2[j]) * slope
        b1g[j] = jnp.sum(grad_pre, axis=0, keepdims=True)
        grad_pre_bf = grad_pre.astype(BF16)
        dw1[j] = tn(nm_ref[...], grad_pre_bf)
        gacc[...] += nt(grad_pre_bf, w1[j])
        return carry

    lax.fori_loop(0, CHUNKS, chunk, 0)
    for b in range(IMGS):
        out_ref[b] = (acc[b * PAD : b * PAD + SEQ, :] * live[b]).astype(BF16)

    hat_mid, inv_mid = norm_forward(pad_ref[...])
    grad_normed = gacc[...]
    grad_float = go_ref[...].astype(F32)
    grad_mid = grad_float + norm_backward(grad_normed * vec_ref[:, D : 2 * D], hat_mid, inv_mid)
    gmid_ref[...] = grad_mid
    dwo[...] = tn(att_ref[...], grad_mid.astype(BF16))
    vecg_ref[...] = jnp.zeros((1, GAINS + BIASES), F32)
    vecg_ref[:, D : 2 * D] = jnp.sum(grad_normed * hat_mid, axis=0, keepdims=True)
    base = GAINS
    vecg_ref[:, base + 3 * D : base + 4 * D] = jnp.sum(grad_mid, axis=0, keepdims=True)
    vecg_ref[:, base + 4 * D : base + 5 * D] = jnp.sum(grad_normed, axis=0, keepdims=True)
    for j in range(CHUNKS):
        vecg_ref[:, base + (5 + j) * D : base + (6 + j) * D] = b1g[j]
    vecg_ref[:, base + 5 * D + FF :] = jnp.sum(grad_float, axis=0, keepdims=True)

    def pairs(p, carry):
        rows = pl.ds(pl.multiple_of(p * 2 * STRIPE, 8), 2 * STRIPE)
        for t in range(FC_TILES):
            value = dw1[t // 3, rows, (t % 3) * LANES : (t % 3 + 1) * LANES]
            scatter_rows(flat_ref, p, t, FC_TILES, value)
        for t in range(OUT_TILES):
            scatter_rows(
                flat_ref, p, OUT_START + t, OUT_TILES, dwo[rows, t * LANES : (t + 1) * LANES]
            )
        return carry

    lax.fori_loop(0, BLOCKS // 2, pairs, 0)

    def talls_back(d, carry):
        rows = pl.ds(pl.multiple_of((d & 7) * TALL, 16), TALL)
        for t in range(OUT_TILES):
            flat_ref[d, pl.ds(FC2_START + t, TALL, stride=OUT_TILES), :] = dw2[
                d >> 3, rows, t * LANES : (t + 1) * LANES
            ]
        return carry

    lax.fori_loop(0, BLOCKS, talls_back, 0)
    used = FC2_START + FC_ROWS
    flat_ref[:, used:, :] = jnp.zeros((BLOCKS, SECOND_ROWS - used, LANES), F32)
    pack(me, flat_ref, grads[:4], 0, 0, SECOND_SPLIT[0])
    pack(me, flat_ref, grads[4:], 1, *SECOND_SPLIT)


def back_kernel(
    swaps, counts_ref, x_ref, qkv_ref, gmid_ref, wqkv_ref, wout_ref, vec_ref, vecg_ref, *refs
):
    xgrad_ref = refs[0]
    grads = refs[1:5]
    flat_ref, pad_ref, ga_ref, gp_ref, gpb_ref, dwq, vsum = refs[5:]
    me = position(swaps)
    gmid_bf = gmid_ref[...].astype(BF16)
    ga_ref[...] = nt(gmid_bf, wout_ref[...]).astype(BF16)

    masks = head_masks()
    alive = jnp.where(lax.broadcasted_iota(jnp.int32, (PAD, 1), 0) < SEQ, 0.0, -1e30)

    def image(b, carry):
        rows = pl.ds(pl.multiple_of(b * PAD, 16), PAD)
        for pair in range(HEADS // 2):
            cols = pair * LANES
            q2 = qkv_ref[rows, cols : cols + LANES]
            k2 = qkv_ref[rows, D + cols : D + cols + LANES]
            v2 = qkv_ref[rows, 2 * D + cols : 2 * D + cols + LANES]
            g2 = ga_ref[rows, cols : cols + LANES]
            gq = jnp.zeros((PAD, LANES), F32)
            gk = jnp.zeros((PAD, LANES), F32)
            gv = jnp.zeros((PAD, LANES), F32)
            for mask in masks:
                qm = q2 * mask
                gm = g2 * mask
                scores = nt(k2, qm) * HEAD_DIM ** (-0.5) + alive
                top = jnp.max(scores, axis=0, keepdims=True)
                grown = jnp.exp(scores - top)
                total = jnp.sum(grown, axis=0, keepdims=True)
                probs = grown * (1.0 / total)
                grad_probs = nt(v2, gm)
                row_dot = jnp.sum(probs * grad_probs, axis=0, keepdims=True)
                grad_scores = (probs * (grad_probs - row_dot) * HEAD_DIM ** (-0.5)).astype(BF16)
                gv = gv + nn(probs.astype(BF16), gm)
                gk = gk + nn(grad_scores, qm)
                gq = gq + tn(grad_scores, k2 * mask)
            gp_ref[rows, cols : cols + LANES] = gq
            gp_ref[rows, D + cols : D + cols + LANES] = gk
            gp_ref[rows, 2 * D + cols : 2 * D + cols + LANES] = gv
        return carry

    lax.fori_loop(0, IMGS, image, 0)

    load_padded(x_ref, pad_ref)
    hat_in, inv_in = norm_forward(pad_ref[...])
    normed_in = (hat_in * vec_ref[:, :D] + bias_slice(vec_ref, 0, D)).astype(BF16)
    gpb_ref[...] = gp_ref[...].astype(BF16)
    dwq[...] = tn(normed_in, gpb_ref[...])
    grad_in = nt(gpb_ref[...], wqkv_ref[...])
    images_grad = gmid_ref[...] + norm_backward(grad_in * vec_ref[:, :D], hat_in, inv_in)
    pad_ref[...] = images_grad
    for b in range(IMGS):
        xgrad_ref[b] = pad_ref[b * PAD : b * PAD + SEQ, :].astype(BF16)

    vsum[...] = vecg_ref[...]
    vsum[:, :D] = jnp.sum(grad_in * hat_in, axis=0, keepdims=True)
    vsum[:, GAINS : GAINS + D] = jnp.sum(grad_in, axis=0, keepdims=True)
    vsum[:, GAINS + D : GAINS + 2 * D] = jnp.sum(gp_ref[:, :D], axis=0, keepdims=True)
    vsum[:, GAINS + 2 * D : GAINS + 3 * D] = jnp.sum(gp_ref[:, 2 * D :], axis=0, keepdims=True)

    flat_ref[:, BIAS_ROW:, :] = jnp.zeros((BLOCKS, FIRST_ROWS - BIAS_ROW, LANES), F32)
    flat_ref[:, BIAS_ROW, :] = collect(vsum[:, GAINS:], BIAS_PART, BIASES)
    flat_ref[:, GAIN_ROW, :] = collect(vsum[:, :GAINS], GAIN_PART, GAINS)

    def pairs(p, carry):
        rows = pl.ds(pl.multiple_of(p * 2 * STRIPE, 8), 2 * STRIPE)
        for t in range(QKV_TILES):
            scatter_rows(flat_ref, p, t, QKV_TILES, dwq[rows, t * LANES : (t + 1) * LANES])
        return carry

    lax.fori_loop(0, BLOCKS // 2, pairs, 0)
    pack(me, flat_ref, grads, 0, 0, FIRST_ROWS)


def near_shape(dims, kind):
    return pltpu.VMEM(dims, kind)


def call(kernel, swaps, outs, scratch, cost, *operands):
    specs = [pl.BlockSpec(memory_space=pltpu.SMEM)]
    specs += [pl.BlockSpec(memory_space=pltpu.VMEM)] * (len(operands) - 1)
    operands = [
        pltpu.with_memory_space_constraint(operand, pltpu.VMEM) if operand.ndim == 2
        or operand.shape[0] == 8 else operand
        for operand in operands
    ]
    return pl.pallas_call(
        functools.partial(kernel, swaps),
        out_shape=outs,
        in_specs=specs,
        out_specs=[pl.BlockSpec(memory_space=pltpu.VMEM)] * len(outs),
        scratch_shapes=scratch,
        compiler_params=pltpu.CompilerParams(vmem_limit_bytes=36 * 1024 * 1024),
        cost_estimate=pl.CostEstimate(flops=cost, transcendentals=0, bytes_accessed=4_000_000),
    )(*operands)


def attend(swaps, counts, images, pieces):
    outs = [
        near_shape((D, 3 * D), BF16),
        near_shape((1, GAINS + BIASES), F32),
        near_shape((ROWS, 3 * D), BF16),
        near_shape((ROWS, D), BF16),
    ]
    scratch = [
        pltpu.VMEM((BLOCKS, FIRST_ROWS, LANES), F32),
        pltpu.VMEM((ROWS, D), F32),
    ]
    return call(attend_kernel, swaps, outs, scratch, 5_000_000_000, counts, images, *pieces)


def piece_shapes(*split):
    return [near_shape((8, rows, LANES), BF16) for rows in split for _ in range(4)]


def mlp(swaps, counts, images, upstream, attended, vec, pieces):
    outs = [
        jax.ShapeDtypeStruct((IMGS, SEQ, D), BF16),
        near_shape((ROWS, D), F32),
        near_shape((1, GAINS + BIASES), F32),
        near_shape((D, D), BF16),
    ] + piece_shapes(*SECOND_SPLIT)
    scratch = [
        pltpu.VMEM((BLOCKS, SECOND_ROWS, LANES), F32),
        pltpu.VMEM((CHUNKS, D, D), BF16),
        pltpu.VMEM((CHUNKS, D, D), BF16),
        pltpu.VMEM((CHUNKS, D, D), F32),
        pltpu.VMEM((CHUNKS, D, D), F32),
        pltpu.VMEM((D, D), F32),
        pltpu.VMEM((CHUNKS, 1, D), F32),
        pltpu.VMEM((CHUNKS, 1, D), F32),
        pltpu.VMEM((ROWS, D), F32),
        pltpu.VMEM((ROWS, D), BF16),
        pltpu.VMEM((ROWS, D), BF16),
        pltpu.VMEM((ROWS, D), F32),
        pltpu.VMEM((ROWS, D), F32),
    ]
    return call(
        mlp_kernel, swaps, outs, scratch, 8_000_000_000,
        counts, images, upstream, attended, vec, *pieces,
    )


def back(swaps, counts, images, qkv, grad_mid, w_qkv, w_out, vec, vec_grad):
    outs = [jax.ShapeDtypeStruct((IMGS, SEQ, D), BF16)] + piece_shapes(FIRST_ROWS)
    scratch = [
        pltpu.VMEM((BLOCKS, FIRST_ROWS, LANES), F32),
        pltpu.VMEM((ROWS, D), F32),
        pltpu.VMEM((ROWS, D), BF16),
        pltpu.VMEM((ROWS, 3 * D), F32),
        pltpu.VMEM((ROWS, 3 * D), BF16),
        pltpu.VMEM((D, 3 * D), F32),
        pltpu.VMEM((1, GAINS + BIASES), F32),
    ]
    return call(
        back_kernel, swaps, outs, scratch, 6_000_000_000,
        counts, images, qkv, grad_mid, w_qkv, w_out, vec, vec_grad,
    )


def exchange(value, mask):
    return lax.ppermute(value, AXES, [(i, i ^ mask) for i in range(BLOCKS)])


def gather_line(block):
    held = block[None]
    for mask in (Z_LOW, Z_HIGH, Y_BIT):
        held = jnp.concatenate([held, exchange(held, mask)])
    other = exchange(held, X_BIT)
    core = exchange(held, CORE_BIT)
    last = exchange(other, CORE_BIT)
    return [held, other, core, last]


def reduce_line(pieces):
    keep, keep_far, send, send_far = pieces
    from_core = exchange(send_far, CORE_BIT)
    far_sum = keep_far.astype(F32) + from_core.astype(F32)
    crossed = exchange(far_sum.astype(BF16), X_BIT)
    from_core = exchange(send, CORE_BIT)
    held = keep.astype(F32) + from_core.astype(F32) + crossed.astype(F32)
    for mask in (Y_BIT, Z_HIGH, Z_LOW):
        half = held.shape[0] // 2
        crossed = exchange(held[half:].astype(BF16), mask)
        held = held[:half] + crossed.astype(F32)
    return held[0]


def gather_blocks(block, split):
    line = [block]
    for mask in (Z_LOW, Z_HIGH, Z_LOW + Z_HIGH):
        line.append(exchange(block, mask))
    colors = []
    for color, (near, far) in enumerate(((Y_BIT, X_BIT), (X_BIT, Y_BIT))):
        part = slice(0, split[0]) if color == 0 else slice(split[0], None)
        first = jnp.stack([piece[part] for piece in line])
        colors.append((first, exchange(first, near), far))
    pieces = []
    for first, second, far in colors:
        plane = jnp.concatenate([first, second])
        other = exchange(plane, far)
        core = exchange(plane, CORE_BIT)
        last = exchange(other, CORE_BIT)
        pieces += [plane, other, core, last]
    return pieces


def reduce_blocks(pieces):
    done = []
    for color, (near, far) in enumerate(((Y_BIT, X_BIT), (X_BIT, Y_BIT))):
        keep, keep_far, send, send_far = pieces[4 * color : 4 * color + 4]
        from_core = exchange(send_far, CORE_BIT)
        far_sum = keep_far.astype(F32) + from_core.astype(F32)
        crossed = exchange(far_sum.astype(BF16), far)
        from_core = exchange(send, CORE_BIT)
        plane = keep.astype(F32) + from_core.astype(F32) + crossed.astype(F32)
        crossed = exchange(plane[4:].astype(BF16), near)
        done.append(plane[:4] + crossed.astype(F32))
    line = jnp.concatenate(done, axis=1)
    total = line[0]
    for step, mask in ((1, Z_LOW), (2, Z_HIGH), (3, Z_LOW + Z_HIGH)):
        crossed = exchange(line[step].astype(BF16), mask)
        total = total + crossed.astype(F32)
    return total


def ordered_pieces(whole, split):
    cube = whole.reshape(2, 2, 4, 2, -1, LANES)
    if len(split) == 1:
        pieces = [cube[x, core].swapaxes(0, 1) for core in range(2) for x in range(2)]
        return [piece.reshape((8,) + piece.shape[2:]) for piece in pieces]
    near, far = cube[..., : split[0], :], cube[..., split[0] :, :]
    pieces = [near[x, core].swapaxes(0, 1) for core in range(2) for x in range(2)]
    pieces += [far[:, core, :, y] for core in range(2) for y in range(2)]
    return [piece.reshape((8,) + piece.shape[2:]) for piece in pieces]


def blocks_of_pieces(pieces):
    first = jnp.stack(pieces[:4]).reshape(2, 2, 2, 4, -1, LANES)
    if len(pieces) == 4:
        return first.transpose(1, 0, 3, 2, 4, 5).reshape(BLOCKS, -1, LANES)
    second = jnp.stack(pieces[4:]).reshape(2, 2, 2, 4, -1, LANES)
    first = first.transpose(1, 0, 3, 2, 4, 5)
    second = second.transpose(2, 0, 3, 1, 4, 5)
    return jnp.concatenate([first, second], axis=4).reshape(BLOCKS, -1, LANES)


def block_rows(flat, rows):
    flat = flat.reshape(flat.shape[:-1] + (-1,))
    short = rows * LANES - flat.shape[-1]
    if short:
        flat = jnp.pad(flat, [(0, 0)] * (flat.ndim - 1) + [(0, short)])
    return flat.reshape(flat.shape[:-1] + (rows, LANES))


def padded_rows(parts, rows):
    short = rows - sum(part.shape[-2] for part in parts)
    filler = jnp.zeros(parts[0].shape[:-2] + (short, LANES), parts[0].dtype)
    return jnp.concatenate([*parts, filler], axis=-2)


def build_first(qkv, gains, biases):
    parts = [block_rows(qkv, QKV_ROWS), block_rows(biases, 1), block_rows(gains, 1)]
    return padded_rows(parts, FIRST_ROWS)


def build_second(out, fc1, fc2):
    parts = [block_rows(fc1, FC_ROWS), block_rows(out, OUT_ROWS), block_rows(fc2, FC_ROWS)]
    return padded_rows(parts, SECOND_ROWS)


def flat_rows(block, start, rows):
    return block[..., start : start + rows, :].reshape(block.shape[:-2] + (-1,))


def split_blocks(first, second):
    return (
        flat_rows(first, 0, QKV_ROWS),
        flat_rows(second, OUT_START, OUT_ROWS),
        flat_rows(second, 0, FC_ROWS),
        flat_rows(second, FC2_START, FC_ROWS),
        first[..., GAIN_ROW, :GAIN_PART],
        first[..., BIAS_ROW, :BIAS_PART],
    )


def adam_update(weight, gradient, moment_one, moment_two, step_rate, decayed):
    first_new = BETA_ONE * moment_one + (1.0 - BETA_ONE) * gradient
    second_new = BETA_TWO * moment_two + (1.0 - BETA_TWO) * gradient * gradient
    first_hat = first_new / (1.0 - BETA_ONE**ADAM_STEP)
    second_hat = second_new / (1.0 - BETA_TWO**ADAM_STEP)
    change = first_hat / (jnp.sqrt(second_hat) + ADAM_EPS)
    if decayed:
        change = change + DECAY_RATE * weight
    return (weight - step_rate * change, first_new, second_new)


def device_step(devices, images, counts, upstream, *state):
    masters, firsts, seconds = state[:6], state[6:12], state[12:18]
    lowered = [master.astype(BF16) for master in masters]
    swaps = devices == BLOCKS
    if swaps:
        qkv, out, fc1, fc2, gains, biases = lowered
        first = gather_line(build_first(qkv, gains, biases))
        second = gather_blocks(build_second(out, fc1, fc2), SECOND_SPLIT)
    else:
        qkv, out, fc1, fc2, gains, biases = [
            lax.all_gather(part, AXES, axis=0, tiled=True).reshape(BLOCKS, -1) for part in lowered
        ]
        first = ordered_pieces(build_first(qkv, gains, biases), (FIRST_ROWS,))
        second = ordered_pieces(build_second(out, fc1, fc2), SECOND_SPLIT)
    w_qkv, vec, qkv, attended = attend(swaps, counts, images, first)
    block_out, grad_mid, vec_grad, w_out, *second_grads = mlp(
        swaps, counts, images, upstream, attended, vec, second
    )
    images_grad, *first_grads = back(
        swaps, counts, images, qkv, grad_mid, w_qkv, w_out, vec, vec_grad
    )
    if swaps:
        second_sum = reduce_blocks(second_grads)
        first_sum = reduce_line(first_grads)
        owned = split_blocks(first_sum, second_sum)
    else:
        owned = tuple(
            lax.psum_scatter(part.reshape(-1), AXES, scatter_dimension=0, tiled=True)
            for part in split_blocks(
                blocks_of_pieces(first_grads).astype(F32),
                blocks_of_pieces(second_grads).astype(F32),
            )
        )
    updates = [
        adam_update(masters[p], owned[p], firsts[p], seconds[p], RATES[p], DECAYED[p])
        for p in range(6)
    ]
    return (
        block_out,
        images_grad,
        *owned,
        *(update[0] for update in updates),
        *(update[1] for update in updates),
        *(update[2] for update in updates),
    )


def solution(mesh):
    devices = math.prod(mesh.shape.values())
    slots = P(AXES, None, None)
    flat = P(AXES)

    def step(*args):
        return device_step(devices, *args)

    return jax.shard_map(
        step,
        mesh=mesh,
        in_specs=(slots, P(), slots) + (flat,) * 18,
        out_specs=(slots, slots) + (flat,) * 24,
        check_vma=False,
    )
```

```python
import functools
import math

import jax
import jax.numpy as jnp
from jax import lax
from jax.experimental import pallas as pl
from jax.experimental.pallas import tpu as pltpu
from jax.sharding import PartitionSpec as P

D = 384
HEADS = 6
HEAD_DIM = 64
FF = 1536
SEQ = 197
ADAM_STEP = 3

NORM_EPS = 1e-06
BETA_ONE = 0.9
BETA_TWO = 0.95
ADAM_EPS = 1e-08
DECAY_RATE = 0.1
RATES = (0.01, 0.05, 0.01, 0.01, 0.2, 0.2)
DECAYED = (True, True, True, True, False, False)
INV_ROOT_TWO = 0.7071067811865476
INV_ROOT_TWOPI = 0.3989422804014327

AXES = ("row", "col")
F32 = jnp.float32
BF16 = jnp.bfloat16
LANES = 128
PAD = 208
IMGS = 2
ROWS = IMGS * PAD
BLOCKS = 32
STRIPE = D // BLOCKS
QKV_TILES = 3 * D // LANES
OUT_TILES = D // LANES
FC_TILES = FF // LANES
QKV_ROWS = STRIPE * QKV_TILES
OUT_ROWS = STRIPE * OUT_TILES
FC_ROWS = STRIPE * FC_TILES
TALL = FF // BLOCKS
BIAS_ROW = QKV_ROWS
GAIN_ROW = BIAS_ROW + 1
FIRST_ROWS = 112
SECOND_ROWS = 336
GATHER_SPLIT = (144, 192)
SUM_SPLIT = (192, 144)
OUT_START = FC_ROWS
FC2_START = OUT_START + OUT_ROWS
GAINS = 2 * D
BIASES = 6 * D + FF
GAIN_PART = GAINS // BLOCKS
BIAS_PART = BIASES // BLOCKS
CHUNKS = FF // D
Y_BIT, Z_LOW, Z_HIGH, CORE_BIT, X_BIT = 1, 2, 4, 8, 16
LINE = (Z_LOW, Z_HIGH, Z_LOW + Z_HIGH)


def nn(a, b):
    return jnp.dot(a, b, preferred_element_type=F32)


def nt(a, b):
    return lax.dot_general(a, b, (((1,), (1,)), ((), ())), preferred_element_type=F32)


def tn(a, b):
    return lax.dot_general(a, b, (((0,), (0,)), ((), ())), preferred_element_type=F32)


def norm_forward(row_data):
    centered = row_data - jnp.mean(row_data, axis=-1, keepdims=True)
    inv_std = lax.rsqrt(jnp.mean(centered * centered, axis=-1, keepdims=True) + NORM_EPS)
    return (centered * inv_std, inv_std)


def norm_backward(grad_hat, normed, inv_std):
    return inv_std * (
        grad_hat
        - jnp.mean(grad_hat, axis=-1, keepdims=True)
        - normed * jnp.mean(grad_hat * normed, axis=-1, keepdims=True)
    )


def masks_of(index, color):
    return (index & 3) * Z_LOW + (index >> 2) * (Y_BIT if color == 0 else X_BIT)


def variants(color):
    last = X_BIT if color == 0 else Y_BIT
    return (0, last, CORE_BIT, last + CORE_BIT)


def unpack(me, piece_refs, flat_ref, color, start, count):
    for piece_ref, extra in zip(piece_refs, variants(color)):

        def body(i, carry, piece_ref=piece_ref, extra=extra):
            owner = me ^ (masks_of(i, color) ^ extra)
            flat_ref[owner, start : start + count, :] = piece_ref[i].astype(F32)
            return carry

        lax.fori_loop(0, 8, body, 0)


def pack(me, grad_ref, out_refs, color, start, count):
    for out_ref, extra in zip(out_refs, variants(color)):

        def body(i, carry, out_ref=out_ref, extra=extra):
            owner = me ^ (masks_of(i, color) ^ extra)
            out_ref[i] = grad_ref[owner, start : start + count, :].astype(BF16)
            return carry

        lax.fori_loop(0, 8, body, 0)


def striped_rows(flat_ref, quad, start, stride):
    parts = [flat_ref[4 * quad + u, pl.ds(start, STRIPE, stride=stride), :] for u in range(4)]
    return jnp.concatenate(parts, axis=0).astype(BF16)


def scatter_rows(flat_ref, pair, start, stride, value):
    for u in range(2):
        flat_ref[2 * pair + u, pl.ds(start, STRIPE, stride=stride), :] = value[
            u * STRIPE : (u + 1) * STRIPE
        ]


def select_matrix(part, total):
    lane = lax.broadcasted_iota(jnp.int32, (LANES, total), 1)
    sub = lax.broadcasted_iota(jnp.int32, (LANES, total), 0)
    block = (lane * ((1 << 22) // part + 1)) >> 22
    return jnp.where(lane - block * part == sub, 1.0, 0.0).astype(BF16)


def owner_mask(part, total):
    lane = lax.broadcasted_iota(jnp.int32, (BLOCKS, total), 1)
    block = lax.broadcasted_iota(jnp.int32, (BLOCKS, total), 0)
    return (lane >= block * part) & (lane < block * part + part)


def spread(block_rows, part, total):
    moved = nn(block_rows.astype(BF16), select_matrix(part, total))
    return jnp.sum(jnp.where(owner_mask(part, total), moved, 0.0), axis=0, keepdims=True)


def collect(row, part, total):
    own = jnp.where(owner_mask(part, total), jnp.broadcast_to(row, (BLOCKS, total)), 0.0)
    return nt(own.astype(BF16), select_matrix(part, total))


def load_padded(x_ref, padded_ref, scales=None):
    for b in range(IMGS):
        tail = (SEQ // 16) * 16
        padded_ref[b * PAD + tail : (b + 1) * PAD, :] = jnp.zeros((PAD - tail, D), F32)
        value = x_ref[b].astype(F32)
        if scales is not None:
            value = value * scales[b]
        padded_ref[b * PAD : b * PAD + SEQ, :] = value


def bias_slice(vec_ref, start, size):
    return vec_ref[:, GAINS + start : GAINS + start + size]


def head_masks():
    lane = lax.broadcasted_iota(jnp.int32, (1, LANES), 1)
    low = jnp.where(lane < HEAD_DIM, 1.0, 0.0)
    return (low.astype(BF16), (1.0 - low).astype(BF16))


def position(swaps):
    return lax.axis_index(AXES) if swaps else jnp.int32(0)


def attend_kernel(swaps, counts_ref, x_ref, *refs):
    pieces = refs[:4]
    wqkv_ref, vec_ref, qkv_ref, att_ref = refs[4:8]
    flat_ref, pad_ref = refs[8:]
    me = position(swaps)
    unpack(me, pieces, flat_ref, 0, 0, FIRST_ROWS)

    def quads(quad, carry):
        rows = pl.ds(pl.multiple_of(quad * 4 * STRIPE, 16), 4 * STRIPE)
        for t in range(QKV_TILES):
            wqkv_ref[rows, t * LANES : (t + 1) * LANES] = striped_rows(
                flat_ref, quad, t, QKV_TILES
            )
        return carry

    lax.fori_loop(0, BLOCKS // 4, quads, 0)
    vec_ref[:, :GAINS] = spread(flat_ref[:, GAIN_ROW, :], GAIN_PART, GAINS)
    vec_ref[:, GAINS:] = spread(flat_ref[:, BIAS_ROW, :], BIAS_PART, BIASES)

    load_padded(x_ref, pad_ref)
    hat_in, _ = norm_forward(pad_ref[...])
    normed_in = (hat_in * vec_ref[:, :D] + bias_slice(vec_ref, 0, D)).astype(BF16)
    qkv_ref[:, :D] = (
        nn(normed_in, wqkv_ref[:, :D]) + bias_slice(vec_ref, D, D)
    ).astype(BF16)
    qkv_ref[:, D : 2 * D] = nn(normed_in, wqkv_ref[:, D : 2 * D]).astype(BF16)
    qkv_ref[:, 2 * D :] = (
        nn(normed_in, wqkv_ref[:, 2 * D :]) + bias_slice(vec_ref, 2 * D, D)
    ).astype(BF16)

    masks = head_masks()
    lane = lax.broadcasted_iota(jnp.int32, (1, LANES), 1)
    dead = jnp.where(lax.broadcasted_iota(jnp.int32, (1, PAD), 1) < SEQ, 0.0, -1e30)

    def image(b, carry):
        rows = pl.ds(pl.multiple_of(b * PAD, 16), PAD)
        for pair in range(HEADS // 2):
            cols = pair * LANES
            q2 = qkv_ref[rows, cols : cols + LANES]
            k2 = qkv_ref[rows, D + cols : D + cols + LANES]
            v2 = qkv_ref[rows, 2 * D + cols : 2 * D + cols + LANES]
            outs = []
            for mask in masks:
                scores = nt(q2 * mask, k2) * HEAD_DIM ** (-0.5) + dead
                top = jnp.max(scores, axis=-1, keepdims=True)
                grown = jnp.exp(scores - top)
                total = jnp.sum(grown, axis=-1, keepdims=True)
                probs = (grown * (1.0 / total)).astype(BF16)
                outs.append(nn(probs, v2))
            att_ref[rows, cols : cols + LANES] = jnp.where(
                lane < HEAD_DIM, outs[0], outs[1]
            ).astype(BF16)
        return carry

    lax.fori_loop(0, IMGS, image, 0)


def mlp_kernel(swaps, counts_ref, x_ref, up_ref, att_ref, vec_ref, *refs):
    pieces = refs[:8]
    out_ref, gmid_ref, vecg_ref, wout_ref = refs[8:12]
    grads = refs[12:20]
    flat_ref, w1, w2, dw1, dw2, dwo, b1, b1g, pad_ref, go_ref, nm_ref, acc, gacc = refs[20:]
    me = position(swaps)
    count = counts_ref[lax.axis_index(AXES)]
    live = [jnp.where(count > b, 1.0, 0.0).astype(F32) for b in range(IMGS)]
    unpack(me, pieces[:4], flat_ref, 0, 0, GATHER_SPLIT[0])
    unpack(me, pieces[4:], flat_ref, 1, *GATHER_SPLIT)

    def quads(quad, carry):
        rows = pl.ds(pl.multiple_of(quad * 4 * STRIPE, 16), 4 * STRIPE)
        for t in range(FC_TILES):
            w1[t // 3, rows, (t % 3) * LANES : (t % 3 + 1) * LANES] = striped_rows(
                flat_ref, quad, t, FC_TILES
            )
        for t in range(OUT_TILES):
            wout_ref[rows, t * LANES : (t + 1) * LANES] = striped_rows(
                flat_ref, quad, OUT_START + t, OUT_TILES
            )
        return carry

    lax.fori_loop(0, BLOCKS // 4, quads, 0)

    def talls(d, carry):
        rows = pl.ds(pl.multiple_of((d & 7) * TALL, 16), TALL)
        for t in range(OUT_TILES):
            w2[d >> 3, rows, t * LANES : (t + 1) * LANES] = flat_ref[
                d, pl.ds(FC2_START + t, TALL, stride=OUT_TILES), :
            ].astype(BF16)
        return carry

    lax.fori_loop(0, BLOCKS, talls, 0)
    for j in range(CHUNKS):
        b1[j] = bias_slice(vec_ref, 5 * D + j * D, D)

    load_padded(x_ref, pad_ref)
    load_padded(up_ref, acc, live)
    go_ref[...] = acc[...].astype(BF16)
    mid = pad_ref[...] + nn(att_ref[...], wout_ref[...]) + bias_slice(vec_ref, 3 * D, D)
    hat_mid, inv_mid = norm_forward(mid)
    nm_ref[...] = (hat_mid * vec_ref[:, D : 2 * D] + bias_slice(vec_ref, 4 * D, D)).astype(BF16)
    acc[...] = mid + bias_slice(vec_ref, 5 * D + FF, D)
    pad_ref[...] = mid
    gacc[...] = jnp.zeros((ROWS, D), F32)

    def chunk(j, carry):
        hidden = nn(nm_ref[...], w1[j]) + b1[j]
        cdf = 0.5 * (1.0 + lax.erf(hidden * INV_ROOT_TWO))
        act = (hidden * cdf).astype(BF16)
        slope = cdf + hidden * INV_ROOT_TWOPI * jnp.exp(-0.5 * hidden * hidden)
        acc[...] += nn(act, w2[j])
        dw2[j] = tn(act, go_ref[...])
        grad_pre = nt(go_ref[...], w2[j]) * slope
        b1g[j] = jnp.sum(grad_pre, axis=0, keepdims=True)
        grad_pre_bf = grad_pre.astype(BF16)
        dw1[j] = tn(nm_ref[...], grad_pre_bf)
        gacc[...] += nt(grad_pre_bf, w1[j])
        return carry

    lax.fori_loop(0, CHUNKS, chunk, 0)
    for b in range(IMGS):
        out_ref[b] = (acc[b * PAD : b * PAD + SEQ, :] * live[b]).astype(BF16)

    hat_mid, inv_mid = norm_forward(pad_ref[...])
    grad_normed = gacc[...]
    grad_float = go_ref[...].astype(F32)
    grad_mid = grad_float + norm_backward(grad_normed * vec_ref[:, D : 2 * D], hat_mid, inv_mid)
    gmid_ref[...] = grad_mid
    dwo[...] = tn(att_ref[...], grad_mid.astype(BF16))
    vecg_ref[...] = jnp.zeros((1, GAINS + BIASES), F32)
    vecg_ref[:, D : 2 * D] = jnp.sum(grad_normed * hat_mid, axis=0, keepdims=True)
    base = GAINS
    vecg_ref[:, base + 3 * D : base + 4 * D] = jnp.sum(grad_mid, axis=0, keepdims=True)
    vecg_ref[:, base + 4 * D : base + 5 * D] = jnp.sum(grad_normed, axis=0, keepdims=True)
    for j in range(CHUNKS):
        vecg_ref[:, base + (5 + j) * D : base + (6 + j) * D] = b1g[j]
    vecg_ref[:, base + 5 * D + FF :] = jnp.sum(grad_float, axis=0, keepdims=True)

    def pairs(p, carry):
        rows = pl.ds(pl.multiple_of(p * 2 * STRIPE, 8), 2 * STRIPE)
        for t in range(FC_TILES):
            value = dw1[t // 3, rows, (t % 3) * LANES : (t % 3 + 1) * LANES]
            scatter_rows(flat_ref, p, t, FC_TILES, value)
        for t in range(OUT_TILES):
            scatter_rows(
                flat_ref, p, OUT_START + t, OUT_TILES, dwo[rows, t * LANES : (t + 1) * LANES]
            )
        return carry

    lax.fori_loop(0, BLOCKS // 2, pairs, 0)

    def talls_back(d, carry):
        rows = pl.ds(pl.multiple_of((d & 7) * TALL, 16), TALL)
        for t in range(OUT_TILES):
            flat_ref[d, pl.ds(FC2_START + t, TALL, stride=OUT_TILES), :] = dw2[
                d >> 3, rows, t * LANES : (t + 1) * LANES
            ]
        return carry

    lax.fori_loop(0, BLOCKS, talls_back, 0)
    used = FC2_START + FC_ROWS
    flat_ref[:, used:, :] = jnp.zeros((BLOCKS, SECOND_ROWS - used, LANES), F32)
    pack(me, flat_ref, grads[:4], 0, 0, SUM_SPLIT[0])
    pack(me, flat_ref, grads[4:], 1, *SUM_SPLIT)


def back_kernel(
    swaps, counts_ref, x_ref, qkv_ref, gmid_ref, wqkv_ref, wout_ref, vec_ref, vecg_ref, *refs
):
    xgrad_ref = refs[0]
    grads = refs[1:5]
    flat_ref, pad_ref, ga_ref, gp_ref, gpb_ref, dwq, vsum = refs[5:]
    me = position(swaps)
    gmid_bf = gmid_ref[...].astype(BF16)
    ga_ref[...] = nt(gmid_bf, wout_ref[...]).astype(BF16)

    masks = head_masks()
    alive = jnp.where(lax.broadcasted_iota(jnp.int32, (PAD, 1), 0) < SEQ, 0.0, -1e30)

    def image(b, carry):
        rows = pl.ds(pl.multiple_of(b * PAD, 16), PAD)
        for pair in range(HEADS // 2):
            cols = pair * LANES
            q2 = qkv_ref[rows, cols : cols + LANES]
            k2 = qkv_ref[rows, D + cols : D + cols + LANES]
            v2 = qkv_ref[rows, 2 * D + cols : 2 * D + cols + LANES]
            g2 = ga_ref[rows, cols : cols + LANES]
            gq = jnp.zeros((PAD, LANES), F32)
            gk = jnp.zeros((PAD, LANES), F32)
            gv = jnp.zeros((PAD, LANES), F32)
            for mask in masks:
                qm = q2 * mask
                gm = g2 * mask
                scores = nt(k2, qm) * HEAD_DIM ** (-0.5) + alive
                top = jnp.max(scores, axis=0, keepdims=True)
                grown = jnp.exp(scores - top)
                total = jnp.sum(grown, axis=0, keepdims=True)
                probs = grown * (1.0 / total)
                grad_probs = nt(v2, gm)
                row_dot = jnp.sum(probs * grad_probs, axis=0, keepdims=True)
                grad_scores = (probs * (grad_probs - row_dot) * HEAD_DIM ** (-0.5)).astype(BF16)
                gv = gv + nn(probs.astype(BF16), gm)
                gk = gk + nn(grad_scores, qm)
                gq = gq + tn(grad_scores, k2 * mask)
            gp_ref[rows, cols : cols + LANES] = gq
            gp_ref[rows, D + cols : D + cols + LANES] = gk
            gp_ref[rows, 2 * D + cols : 2 * D + cols + LANES] = gv
        return carry

    lax.fori_loop(0, IMGS, image, 0)

    load_padded(x_ref, pad_ref)
    hat_in, inv_in = norm_forward(pad_ref[...])
    normed_in = (hat_in * vec_ref[:, :D] + bias_slice(vec_ref, 0, D)).astype(BF16)
    gpb_ref[...] = gp_ref[...].astype(BF16)
    dwq[...] = tn(normed_in, gpb_ref[...])
    grad_in = nt(gpb_ref[...], wqkv_ref[...])
    images_grad = gmid_ref[...] + norm_backward(grad_in * vec_ref[:, :D], hat_in, inv_in)
    pad_ref[...] = images_grad
    for b in range(IMGS):
        xgrad_ref[b] = pad_ref[b * PAD : b * PAD + SEQ, :].astype(BF16)

    vsum[...] = vecg_ref[...]
    vsum[:, :D] = jnp.sum(grad_in * hat_in, axis=0, keepdims=True)
    vsum[:, GAINS : GAINS + D] = jnp.sum(grad_in, axis=0, keepdims=True)
    vsum[:, GAINS + D : GAINS + 2 * D] = jnp.sum(gp_ref[:, :D], axis=0, keepdims=True)
    vsum[:, GAINS + 2 * D : GAINS + 3 * D] = jnp.sum(gp_ref[:, 2 * D :], axis=0, keepdims=True)

    flat_ref[:, BIAS_ROW:, :] = jnp.zeros((BLOCKS, FIRST_ROWS - BIAS_ROW, LANES), F32)
    flat_ref[:, BIAS_ROW, :] = collect(vsum[:, GAINS:], BIAS_PART, BIASES)
    flat_ref[:, GAIN_ROW, :] = collect(vsum[:, :GAINS], GAIN_PART, GAINS)

    def pairs(p, carry):
        rows = pl.ds(pl.multiple_of(p * 2 * STRIPE, 8), 2 * STRIPE)
        for t in range(QKV_TILES):
            scatter_rows(flat_ref, p, t, QKV_TILES, dwq[rows, t * LANES : (t + 1) * LANES])
        return carry

    lax.fori_loop(0, BLOCKS // 2, pairs, 0)
    pack(me, flat_ref, grads, 0, 0, FIRST_ROWS)


def near_shape(dims, kind):
    return pltpu.VMEM(dims, kind)


def call(kernel, swaps, outs, scratch, cost, *operands):
    specs = [pl.BlockSpec(memory_space=pltpu.SMEM)]
    specs += [pl.BlockSpec(memory_space=pltpu.VMEM)] * (len(operands) - 1)
    operands = [
        pltpu.with_memory_space_constraint(operand, pltpu.VMEM) if operand.ndim == 2
        or operand.shape[0] == 8 else operand
        for operand in operands
    ]
    return pl.pallas_call(
        functools.partial(kernel, swaps),
        out_shape=outs,
        in_specs=specs,
        out_specs=[pl.BlockSpec(memory_space=pltpu.VMEM)] * len(outs),
        scratch_shapes=scratch,
        compiler_params=pltpu.CompilerParams(vmem_limit_bytes=36 * 1024 * 1024),
        cost_estimate=pl.CostEstimate(flops=cost, transcendentals=0, bytes_accessed=4_000_000),
    )(*operands)


def attend(swaps, counts, images, pieces):
    outs = [
        near_shape((D, 3 * D), BF16),
        near_shape((1, GAINS + BIASES), F32),
        near_shape((ROWS, 3 * D), BF16),
        near_shape((ROWS, D), BF16),
    ]
    scratch = [
        pltpu.VMEM((BLOCKS, FIRST_ROWS, LANES), F32),
        pltpu.VMEM((ROWS, D), F32),
    ]
    return call(attend_kernel, swaps, outs, scratch, 5_000_000_000, counts, images, *pieces)


def piece_shapes(*split):
    return [near_shape((8, rows, LANES), BF16) for rows in split for _ in range(4)]


def mlp(swaps, counts, images, upstream, attended, vec, pieces):
    outs = [
        jax.ShapeDtypeStruct((IMGS, SEQ, D), BF16),
        near_shape((ROWS, D), F32),
        near_shape((1, GAINS + BIASES), F32),
        near_shape((D, D), BF16),
    ] + piece_shapes(*SUM_SPLIT)
    scratch = [
        pltpu.VMEM((BLOCKS, SECOND_ROWS, LANES), F32),
        pltpu.VMEM((CHUNKS, D, D), BF16),
        pltpu.VMEM((CHUNKS, D, D), BF16),
        pltpu.VMEM((CHUNKS, D, D), F32),
        pltpu.VMEM((CHUNKS, D, D), F32),
        pltpu.VMEM((D, D), F32),
        pltpu.VMEM((CHUNKS, 1, D), F32),
        pltpu.VMEM((CHUNKS, 1, D), F32),
        pltpu.VMEM((ROWS, D), F32),
        pltpu.VMEM((ROWS, D), BF16),
        pltpu.VMEM((ROWS, D), BF16),
        pltpu.VMEM((ROWS, D), F32),
        pltpu.VMEM((ROWS, D), F32),
    ]
    return call(
        mlp_kernel, swaps, outs, scratch, 8_000_000_000,
        counts, images, upstream, attended, vec, *pieces,
    )


def back(swaps, counts, images, qkv, grad_mid, w_qkv, w_out, vec, vec_grad):
    outs = [jax.ShapeDtypeStruct((IMGS, SEQ, D), BF16)] + piece_shapes(FIRST_ROWS)
    scratch = [
        pltpu.VMEM((BLOCKS, FIRST_ROWS, LANES), F32),
        pltpu.VMEM((ROWS, D), F32),
        pltpu.VMEM((ROWS, D), BF16),
        pltpu.VMEM((ROWS, 3 * D), F32),
        pltpu.VMEM((ROWS, 3 * D), BF16),
        pltpu.VMEM((D, 3 * D), F32),
        pltpu.VMEM((1, GAINS + BIASES), F32),
    ]
    return call(
        back_kernel, swaps, outs, scratch, 6_000_000_000,
        counts, images, qkv, grad_mid, w_qkv, w_out, vec, vec_grad,
    )


def exchange(value, mask):
    return lax.ppermute(value, AXES, [(i, i ^ mask) for i in range(BLOCKS)])


def gather_line(block):
    line = [block]
    for mask in LINE:
        line.append(exchange(block, mask))
    held = jnp.stack(line)
    held = jnp.concatenate([held, exchange(held, Y_BIT)])
    other = exchange(held, X_BIT)
    core = exchange(held, CORE_BIT)
    last = exchange(other, CORE_BIT)
    return [held, other, core, last]


def reduce_line(pieces):
    keep, keep_far, send, send_far = pieces
    from_core = exchange(send_far, CORE_BIT)
    far_sum = keep_far.astype(F32) + from_core.astype(F32)
    crossed = exchange(far_sum.astype(BF16), X_BIT)
    from_core = exchange(send, CORE_BIT)
    held = keep.astype(F32) + from_core.astype(F32) + crossed.astype(F32)
    crossed = exchange(held[4:].astype(BF16), Y_BIT)
    return sum_line(held[:4] + crossed.astype(F32))


def sum_line(line):
    total = line[0]
    for step, mask in enumerate(LINE):
        crossed = exchange(line[step + 1].astype(BF16), mask)
        total = total + crossed.astype(F32)
    return total


def gather_blocks(block, split):
    line = [block]
    for mask in LINE:
        line.append(exchange(block, mask))
    colors = []
    for color, (near, far) in enumerate(((Y_BIT, X_BIT), (X_BIT, Y_BIT))):
        part = slice(0, split[0]) if color == 0 else slice(split[0], None)
        first = jnp.stack([piece[part] for piece in line])
        colors.append((first, exchange(first, near), far))
    pieces = []
    for first, second, far in colors:
        plane = jnp.concatenate([first, second])
        other = exchange(plane, far)
        core = exchange(plane, CORE_BIT)
        last = exchange(other, CORE_BIT)
        pieces += [plane, other, core, last]
    return pieces


def reduce_blocks(pieces):
    done = []
    for color, (near, far) in enumerate(((Y_BIT, X_BIT), (X_BIT, Y_BIT))):
        keep, keep_far, send, send_far = pieces[4 * color : 4 * color + 4]
        from_core = exchange(send_far, CORE_BIT)
        far_sum = keep_far.astype(F32) + from_core.astype(F32)
        crossed = exchange(far_sum.astype(BF16), far)
        from_core = exchange(send, CORE_BIT)
        plane = keep.astype(F32) + from_core.astype(F32) + crossed.astype(F32)
        crossed = exchange(plane[4:].astype(BF16), near)
        done.append(plane[:4] + crossed.astype(F32))
    line = jnp.concatenate(done, axis=1)
    return sum_line(line)


def ordered_pieces(whole, split):
    cube = whole.reshape(2, 2, 4, 2, -1, LANES)
    if len(split) == 1:
        pieces = [cube[x, core].swapaxes(0, 1) for core in range(2) for x in range(2)]
        return [piece.reshape((8,) + piece.shape[2:]) for piece in pieces]
    near, far = cube[..., : split[0], :], cube[..., split[0] :, :]
    pieces = [near[x, core].swapaxes(0, 1) for core in range(2) for x in range(2)]
    pieces += [far[:, core, :, y] for core in range(2) for y in range(2)]
    return [piece.reshape((8,) + piece.shape[2:]) for piece in pieces]


def blocks_of_pieces(pieces):
    first = jnp.stack(pieces[:4]).reshape(2, 2, 2, 4, -1, LANES)
    if len(pieces) == 4:
        return first.transpose(1, 0, 3, 2, 4, 5).reshape(BLOCKS, -1, LANES)
    second = jnp.stack(pieces[4:]).reshape(2, 2, 2, 4, -1, LANES)
    first = first.transpose(1, 0, 3, 2, 4, 5)
    second = second.transpose(2, 0, 3, 1, 4, 5)
    return jnp.concatenate([first, second], axis=4).reshape(BLOCKS, -1, LANES)


def block_rows(flat, rows):
    flat = flat.reshape(flat.shape[:-1] + (-1,))
    short = rows * LANES - flat.shape[-1]
    if short:
        flat = jnp.pad(flat, [(0, 0)] * (flat.ndim - 1) + [(0, short)])
    return flat.reshape(flat.shape[:-1] + (rows, LANES))


def padded_rows(parts, rows):
    short = rows - sum(part.shape[-2] for part in parts)
    filler = jnp.zeros(parts[0].shape[:-2] + (short, LANES), parts[0].dtype)
    return jnp.concatenate([*parts, filler], axis=-2)


def build_first(qkv, gains, biases):
    parts = [block_rows(qkv, QKV_ROWS), block_rows(biases, 1), block_rows(gains, 1)]
    return padded_rows(parts, FIRST_ROWS)


def build_second(out, fc1, fc2):
    parts = [block_rows(fc1, FC_ROWS), block_rows(out, OUT_ROWS), block_rows(fc2, FC_ROWS)]
    return padded_rows(parts, SECOND_ROWS)


def flat_rows(block, start, rows):
    return block[..., start : start + rows, :].reshape(block.shape[:-2] + (-1,))


def split_blocks(first, second):
    return (
        flat_rows(first, 0, QKV_ROWS),
        flat_rows(second, OUT_START, OUT_ROWS),
        flat_rows(second, 0, FC_ROWS),
        flat_rows(second, FC2_START, FC_ROWS),
        first[..., GAIN_ROW, :GAIN_PART],
        first[..., BIAS_ROW, :BIAS_PART],
    )


def adam_update(weight, gradient, moment_one, moment_two, step_rate, decayed):
    first_new = BETA_ONE * moment_one + (1.0 - BETA_ONE) * gradient
    second_new = BETA_TWO * moment_two + (1.0 - BETA_TWO) * gradient * gradient
    first_hat = first_new / (1.0 - BETA_ONE**ADAM_STEP)
    second_hat = second_new / (1.0 - BETA_TWO**ADAM_STEP)
    change = first_hat / (jnp.sqrt(second_hat) + ADAM_EPS)
    if decayed:
        change = change + DECAY_RATE * weight
    return (weight - step_rate * change, first_new, second_new)


def device_step(devices, images, counts, upstream, *state):
    masters, firsts, seconds = state[:6], state[6:12], state[12:18]
    swaps = devices == BLOCKS
    if swaps:
        qkv, out, fc1, fc2, gains, biases = masters
        first = gather_line(build_first(qkv, gains, biases).astype(BF16))
        second = gather_blocks(build_second(out, fc1, fc2).astype(BF16), GATHER_SPLIT)
    else:
        qkv, out, fc1, fc2, gains, biases = [
            lax.all_gather(part.astype(BF16), AXES, axis=0, tiled=True).reshape(BLOCKS, -1)
            for part in masters
        ]
        first = ordered_pieces(build_first(qkv, gains, biases), (FIRST_ROWS,))
        second = ordered_pieces(build_second(out, fc1, fc2), GATHER_SPLIT)
    w_qkv, vec, qkv, attended = attend(swaps, counts, images, first)
    block_out, grad_mid, vec_grad, w_out, *second_grads = mlp(
        swaps, counts, images, upstream, attended, vec, second
    )
    images_grad, *first_grads = back(
        swaps, counts, images, qkv, grad_mid, w_qkv, w_out, vec, vec_grad
    )
    if swaps:
        second_sum = reduce_blocks(second_grads)
        first_sum = reduce_line(first_grads)
        owned = split_blocks(first_sum, second_sum)
    else:
        owned = tuple(
            lax.psum_scatter(part.reshape(-1), AXES, scatter_dimension=0, tiled=True)
            for part in split_blocks(
                blocks_of_pieces(first_grads).astype(F32),
                blocks_of_pieces(second_grads).astype(F32),
            )
        )
    updates = [
        adam_update(masters[p], owned[p], firsts[p], seconds[p], RATES[p], DECAYED[p])
        for p in range(6)
    ]
    return (
        block_out,
        images_grad,
        *owned,
        *(update[0] for update in updates),
        *(update[1] for update in updates),
        *(update[2] for update in updates),
    )


def solution(mesh):
    devices = math.prod(mesh.shape.values())
    slots = P(AXES, None, None)
    flat = P(AXES)

    def step(*args):
        return device_step(devices, *args)

    return jax.shard_map(
        step,
        mesh=mesh,
        in_specs=(slots, P(), slots) + (flat,) * 18,
        out_specs=(slots, slots) + (flat,) * 24,
        check_vma=False,
    )
```

```python
import functools
import math

import jax
import jax.numpy as jnp
from jax import lax
from jax.experimental import pallas as pl
from jax.experimental.layout import Layout, with_layout_constraint
from jax.experimental.pallas import tpu as pltpu
from jax.sharding import PartitionSpec as P

D = 384
HEADS = 6
HEAD_DIM = 64
FF = 1536
SEQ = 197
ADAM_STEP = 3

NORM_EPS = 1e-06
BETA_ONE = 0.9
BETA_TWO = 0.95
ADAM_EPS = 1e-08
DECAY_RATE = 0.1
RATES = (0.01, 0.05, 0.01, 0.01, 0.2, 0.2)
DECAYED = (True, True, True, True, False, False)
INV_ROOT_TWO = 0.7071067811865476
INV_ROOT_TWOPI = 0.3989422804014327

AXES = ("row", "col")
F32 = jnp.float32
BF16 = jnp.bfloat16
LANES = 128
PAD = 208
IMGS = 2
ROWS = IMGS * PAD
BLOCKS = 32
STRIPE = D // BLOCKS
QKV_TILES = 3 * D // LANES
OUT_TILES = D // LANES
FC_TILES = FF // LANES
QKV_ROWS = STRIPE * QKV_TILES
OUT_ROWS = STRIPE * OUT_TILES
FC_ROWS = STRIPE * FC_TILES
TALL = FF // BLOCKS
BIAS_ROW = QKV_ROWS
GAIN_ROW = BIAS_ROW + 1
FIRST_ROWS = 112
SECOND_ROWS = 336
GATHER_SPLIT = (144, 192)
SUM_SPLIT = (192, 144)
OUT_START = FC_ROWS
FC2_START = OUT_START + OUT_ROWS
GAINS = 2 * D
BIASES = 6 * D + FF
GAIN_PART = GAINS // BLOCKS
BIAS_PART = BIASES // BLOCKS
CHUNKS = FF // D
Y_BIT, Z_LOW, Z_HIGH, CORE_BIT, X_BIT = 1, 2, 4, 8, 16
TOKEN_MAJOR = Layout(major_to_minor=(1, 0, 2))
LINE = (Z_LOW, Z_HIGH, Z_LOW + Z_HIGH)


def nn(a, b):
    return jnp.dot(a, b, preferred_element_type=F32)


def nt(a, b):
    return lax.dot_general(a, b, (((1,), (1,)), ((), ())), preferred_element_type=F32)


def tn(a, b):
    return lax.dot_general(a, b, (((0,), (0,)), ((), ())), preferred_element_type=F32)


def norm_forward(row_data):
    centered = row_data - jnp.mean(row_data, axis=-1, keepdims=True)
    inv_std = lax.rsqrt(jnp.mean(centered * centered, axis=-1, keepdims=True) + NORM_EPS)
    return (centered * inv_std, inv_std)


def norm_backward(grad_hat, normed, inv_std):
    return inv_std * (
        grad_hat
        - jnp.mean(grad_hat, axis=-1, keepdims=True)
        - normed * jnp.mean(grad_hat * normed, axis=-1, keepdims=True)
    )


def masks_of(index, color):
    return (index & 3) * Z_LOW + (index >> 2) * (Y_BIT if color == 0 else X_BIT)


def variants(color):
    last = X_BIT if color == 0 else Y_BIT
    return (0, last, CORE_BIT, last + CORE_BIT)


def unpack(me, piece_refs, flat_ref, color, start, count):
    for piece_ref, extra in zip(piece_refs, variants(color)):

        def body(i, carry, piece_ref=piece_ref, extra=extra):
            owner = me ^ (masks_of(i, color) ^ extra)
            flat_ref[owner, start : start + count, :] = piece_ref[i].astype(F32)
            return carry

        lax.fori_loop(0, 8, body, 0)


def pack(me, grad_ref, out_refs, color, start, count):
    for out_ref, extra in zip(out_refs, variants(color)):

        def body(i, carry, out_ref=out_ref, extra=extra):
            owner = me ^ (masks_of(i, color) ^ extra)
            out_ref[i] = grad_ref[owner, start : start + count, :].astype(BF16)
            return carry

        lax.fori_loop(0, 8, body, 0)


def striped_rows(flat_ref, quad, start, stride):
    parts = [flat_ref[4 * quad + u, pl.ds(start, STRIPE, stride=stride), :] for u in range(4)]
    return jnp.concatenate(parts, axis=0).astype(BF16)


def scatter_rows(flat_ref, pair, start, stride, value):
    for u in range(2):
        flat_ref[2 * pair + u, pl.ds(start, STRIPE, stride=stride), :] = value[
            u * STRIPE : (u + 1) * STRIPE
        ]


def select_matrix(part, total):
    lane = lax.broadcasted_iota(jnp.int32, (LANES, total), 1)
    sub = lax.broadcasted_iota(jnp.int32, (LANES, total), 0)
    block = (lane * ((1 << 22) // part + 1)) >> 22
    return jnp.where(lane - block * part == sub, 1.0, 0.0).astype(BF16)


def owner_mask(part, total):
    lane = lax.broadcasted_iota(jnp.int32, (BLOCKS, total), 1)
    block = lax.broadcasted_iota(jnp.int32, (BLOCKS, total), 0)
    return (lane >= block * part) & (lane < block * part + part)


def spread(block_rows, part, total):
    moved = nn(block_rows.astype(BF16), select_matrix(part, total))
    return jnp.sum(jnp.where(owner_mask(part, total), moved, 0.0), axis=0, keepdims=True)


def collect(row, part, total):
    own = jnp.where(owner_mask(part, total), jnp.broadcast_to(row, (BLOCKS, total)), 0.0)
    return nt(own.astype(BF16), select_matrix(part, total))


def load_padded(x_ref, padded_ref, scales=None):
    for b in range(IMGS):
        tail = (SEQ // 16) * 16
        padded_ref[b * PAD + tail : (b + 1) * PAD, :] = jnp.zeros((PAD - tail, D), F32)
        value = x_ref[b].astype(F32)
        if scales is not None:
            value = value * scales[b]
        padded_ref[b * PAD : b * PAD + SEQ, :] = value


def bias_slice(vec_ref, start, size):
    return vec_ref[:, GAINS + start : GAINS + start + size]


def head_masks():
    lane = lax.broadcasted_iota(jnp.int32, (1, LANES), 1)
    low = jnp.where(lane < HEAD_DIM, 1.0, 0.0)
    return (low.astype(BF16), (1.0 - low).astype(BF16))


def position(swaps):
    return lax.axis_index(AXES) if swaps else jnp.int32(0)


def attend_kernel(swaps, counts_ref, x_ref, *refs):
    pieces = refs[:4]
    wqkv_ref, vec_ref, qkv_ref, att_ref = refs[4:8]
    flat_ref, pad_ref = refs[8:]
    me = position(swaps)
    unpack(me, pieces, flat_ref, 0, 0, FIRST_ROWS)

    def quads(quad, carry):
        rows = pl.ds(pl.multiple_of(quad * 4 * STRIPE, 16), 4 * STRIPE)
        for t in range(QKV_TILES):
            wqkv_ref[rows, t * LANES : (t + 1) * LANES] = striped_rows(
                flat_ref, quad, t, QKV_TILES
            )
        return carry

    lax.fori_loop(0, BLOCKS // 4, quads, 0)
    vec_ref[:, :GAINS] = spread(flat_ref[:, GAIN_ROW, :], GAIN_PART, GAINS)
    vec_ref[:, GAINS:] = spread(flat_ref[:, BIAS_ROW, :], BIAS_PART, BIASES)

    load_padded(x_ref, pad_ref)
    hat_in, _ = norm_forward(pad_ref[...])
    normed_in = (hat_in * vec_ref[:, :D] + bias_slice(vec_ref, 0, D)).astype(BF16)
    qkv_ref[:, :D] = (
        nn(normed_in, wqkv_ref[:, :D]) + bias_slice(vec_ref, D, D)
    ).astype(BF16)
    qkv_ref[:, D : 2 * D] = nn(normed_in, wqkv_ref[:, D : 2 * D]).astype(BF16)
    qkv_ref[:, 2 * D :] = (
        nn(normed_in, wqkv_ref[:, 2 * D :]) + bias_slice(vec_ref, 2 * D, D)
    ).astype(BF16)

    masks = head_masks()
    lane = lax.broadcasted_iota(jnp.int32, (1, LANES), 1)
    dead = jnp.where(lax.broadcasted_iota(jnp.int32, (1, PAD), 1) < SEQ, 0.0, -1e30)

    def image(b, carry):
        rows = pl.ds(pl.multiple_of(b * PAD, 16), PAD)
        for pair in range(HEADS // 2):
            cols = pair * LANES
            q2 = qkv_ref[rows, cols : cols + LANES]
            k2 = qkv_ref[rows, D + cols : D + cols + LANES]
            v2 = qkv_ref[rows, 2 * D + cols : 2 * D + cols + LANES]
            outs = []
            for mask in masks:
                scores = nt(q2 * mask, k2) * HEAD_DIM ** (-0.5) + dead
                top = jnp.max(scores, axis=-1, keepdims=True)
                grown = jnp.exp(scores - top)
                total = jnp.sum(grown, axis=-1, keepdims=True)
                probs = (grown * (1.0 / total)).astype(BF16)
                outs.append(nn(probs, v2))
            att_ref[rows, cols : cols + LANES] = jnp.where(
                lane < HEAD_DIM, outs[0], outs[1]
            ).astype(BF16)
        return carry

    lax.fori_loop(0, IMGS, image, 0)


def mlp_kernel(swaps, counts_ref, x_ref, up_ref, att_ref, vec_ref, *refs):
    pieces = refs[:8]
    out_ref, gmid_ref, vecg_ref, wout_ref = refs[8:12]
    grads = refs[12:20]
    flat_ref, w1, w2, dw1, dw2, dwo, b1, b1g, pad_ref, go_ref, nm_ref, acc, gacc = refs[20:]
    me = position(swaps)
    count = counts_ref[lax.axis_index(AXES)]
    live = [jnp.where(count > b, 1.0, 0.0).astype(F32) for b in range(IMGS)]
    unpack(me, pieces[:4], flat_ref, 0, 0, GATHER_SPLIT[0])
    unpack(me, pieces[4:], flat_ref, 1, *GATHER_SPLIT)

    def quads(quad, carry):
        rows = pl.ds(pl.multiple_of(quad * 4 * STRIPE, 16), 4 * STRIPE)
        for t in range(FC_TILES):
            w1[t // 3, rows, (t % 3) * LANES : (t % 3 + 1) * LANES] = striped_rows(
                flat_ref, quad, t, FC_TILES
            )
        for t in range(OUT_TILES):
            wout_ref[rows, t * LANES : (t + 1) * LANES] = striped_rows(
                flat_ref, quad, OUT_START + t, OUT_TILES
            )
        return carry

    lax.fori_loop(0, BLOCKS // 4, quads, 0)

    def talls(d, carry):
        rows = pl.ds(pl.multiple_of((d & 7) * TALL, 16), TALL)
        for t in range(OUT_TILES):
            w2[d >> 3, rows, t * LANES : (t + 1) * LANES] = flat_ref[
                d, pl.ds(FC2_START + t, TALL, stride=OUT_TILES), :
            ].astype(BF16)
        return carry

    lax.fori_loop(0, BLOCKS, talls, 0)
    for j in range(CHUNKS):
        b1[j] = bias_slice(vec_ref, 5 * D + j * D, D)

    load_padded(x_ref, pad_ref)
    load_padded(up_ref, acc, live)
    go_ref[...] = acc[...].astype(BF16)
    mid = pad_ref[...] + nn(att_ref[...], wout_ref[...]) + bias_slice(vec_ref, 3 * D, D)
    hat_mid, inv_mid = norm_forward(mid)
    nm_ref[...] = (hat_mid * vec_ref[:, D : 2 * D] + bias_slice(vec_ref, 4 * D, D)).astype(BF16)
    acc[...] = mid + bias_slice(vec_ref, 5 * D + FF, D)
    pad_ref[...] = mid
    gacc[...] = jnp.zeros((ROWS, D), F32)

    def chunk(j, carry):
        hidden = nn(nm_ref[...], w1[j]) + b1[j]
        cdf = 0.5 * (1.0 + lax.erf(hidden * INV_ROOT_TWO))
        act = (hidden * cdf).astype(BF16)
        slope = cdf + hidden * INV_ROOT_TWOPI * jnp.exp(-0.5 * hidden * hidden)
        acc[...] += nn(act, w2[j])
        dw2[j] = tn(act, go_ref[...])
        grad_pre = nt(go_ref[...], w2[j]) * slope
        b1g[j] = jnp.sum(grad_pre, axis=0, keepdims=True)
        grad_pre_bf = grad_pre.astype(BF16)
        dw1[j] = tn(nm_ref[...], grad_pre_bf)
        gacc[...] += nt(grad_pre_bf, w1[j])
        return carry

    lax.fori_loop(0, CHUNKS, chunk, 0)
    for b in range(IMGS):
        out_ref[b] = (acc[b * PAD : b * PAD + SEQ, :] * live[b]).astype(BF16)

    hat_mid, inv_mid = norm_forward(pad_ref[...])
    grad_normed = gacc[...]
    grad_float = go_ref[...].astype(F32)
    grad_mid = grad_float + norm_backward(grad_normed * vec_ref[:, D : 2 * D], hat_mid, inv_mid)
    gmid_ref[...] = grad_mid
    dwo[...] = tn(att_ref[...], grad_mid.astype(BF16))
    vecg_ref[...] = jnp.zeros((1, GAINS + BIASES), F32)
    vecg_ref[:, D : 2 * D] = jnp.sum(grad_normed * hat_mid, axis=0, keepdims=True)
    base = GAINS
    vecg_ref[:, base + 3 * D : base + 4 * D] = jnp.sum(grad_mid, axis=0, keepdims=True)
    vecg_ref[:, base + 4 * D : base + 5 * D] = jnp.sum(grad_normed, axis=0, keepdims=True)
    for j in range(CHUNKS):
        vecg_ref[:, base + (5 + j) * D : base + (6 + j) * D] = b1g[j]
    vecg_ref[:, base + 5 * D + FF :] = jnp.sum(grad_float, axis=0, keepdims=True)

    def pairs(p, carry):
        rows = pl.ds(pl.multiple_of(p * 2 * STRIPE, 8), 2 * STRIPE)
        for t in range(FC_TILES):
            value = dw1[t // 3, rows, (t % 3) * LANES : (t % 3 + 1) * LANES]
            scatter_rows(flat_ref, p, t, FC_TILES, value)
        for t in range(OUT_TILES):
            scatter_rows(
                flat_ref, p, OUT_START + t, OUT_TILES, dwo[rows, t * LANES : (t + 1) * LANES]
            )
        return carry

    lax.fori_loop(0, BLOCKS // 2, pairs, 0)

    def talls_back(d, carry):
        rows = pl.ds(pl.multiple_of((d & 7) * TALL, 16), TALL)
        for t in range(OUT_TILES):
            flat_ref[d, pl.ds(FC2_START + t, TALL, stride=OUT_TILES), :] = dw2[
                d >> 3, rows, t * LANES : (t + 1) * LANES
            ]
        return carry

    lax.fori_loop(0, BLOCKS, talls_back, 0)
    used = FC2_START + FC_ROWS
    flat_ref[:, used:, :] = jnp.zeros((BLOCKS, SECOND_ROWS - used, LANES), F32)
    pack(me, flat_ref, grads[:4], 0, 0, SUM_SPLIT[0])
    pack(me, flat_ref, grads[4:], 1, *SUM_SPLIT)


def back_kernel(
    swaps, counts_ref, x_ref, qkv_ref, gmid_ref, wqkv_ref, wout_ref, vec_ref, vecg_ref, *refs
):
    xgrad_ref = refs[0]
    grads = refs[1:5]
    flat_ref, pad_ref, ga_ref, gp_ref, gpb_ref, dwq, vsum = refs[5:]
    me = position(swaps)
    gmid_bf = gmid_ref[...].astype(BF16)
    ga_ref[...] = nt(gmid_bf, wout_ref[...]).astype(BF16)

    masks = head_masks()
    alive = jnp.where(lax.broadcasted_iota(jnp.int32, (PAD, 1), 0) < SEQ, 0.0, -1e30)

    def image(b, carry):
        rows = pl.ds(pl.multiple_of(b * PAD, 16), PAD)
        for pair in range(HEADS // 2):
            cols = pair * LANES
            q2 = qkv_ref[rows, cols : cols + LANES]
            k2 = qkv_ref[rows, D + cols : D + cols + LANES]
            v2 = qkv_ref[rows, 2 * D + cols : 2 * D + cols + LANES]
            g2 = ga_ref[rows, cols : cols + LANES]
            gq = jnp.zeros((PAD, LANES), F32)
            gk = jnp.zeros((PAD, LANES), F32)
            gv = jnp.zeros((PAD, LANES), F32)
            for mask in masks:
                qm = q2 * mask
                gm = g2 * mask
                scores = nt(k2, qm) * HEAD_DIM ** (-0.5) + alive
                top = jnp.max(scores, axis=0, keepdims=True)
                grown = jnp.exp(scores - top)
                total = jnp.sum(grown, axis=0, keepdims=True)
                probs = grown * (1.0 / total)
                grad_probs = nt(v2, gm)
                row_dot = jnp.sum(probs * grad_probs, axis=0, keepdims=True)
                grad_scores = (probs * (grad_probs - row_dot) * HEAD_DIM ** (-0.5)).astype(BF16)
                gv = gv + nn(probs.astype(BF16), gm)
                gk = gk + nn(grad_scores, qm)
                gq = gq + tn(grad_scores, k2 * mask)
            gp_ref[rows, cols : cols + LANES] = gq
            gp_ref[rows, D + cols : D + cols + LANES] = gk
            gp_ref[rows, 2 * D + cols : 2 * D + cols + LANES] = gv
        return carry

    lax.fori_loop(0, IMGS, image, 0)

    load_padded(x_ref, pad_ref)
    hat_in, inv_in = norm_forward(pad_ref[...])
    normed_in = (hat_in * vec_ref[:, :D] + bias_slice(vec_ref, 0, D)).astype(BF16)
    gpb_ref[...] = gp_ref[...].astype(BF16)
    dwq[...] = tn(normed_in, gpb_ref[...])
    grad_in = nt(gpb_ref[...], wqkv_ref[...])
    images_grad = gmid_ref[...] + norm_backward(grad_in * vec_ref[:, :D], hat_in, inv_in)
    pad_ref[...] = images_grad
    for b in range(IMGS):
        xgrad_ref[b] = pad_ref[b * PAD : b * PAD + SEQ, :].astype(BF16)

    vsum[...] = vecg_ref[...]
    vsum[:, :D] = jnp.sum(grad_in * hat_in, axis=0, keepdims=True)
    vsum[:, GAINS : GAINS + D] = jnp.sum(grad_in, axis=0, keepdims=True)
    vsum[:, GAINS + D : GAINS + 2 * D] = jnp.sum(gp_ref[:, :D], axis=0, keepdims=True)
    vsum[:, GAINS + 2 * D : GAINS + 3 * D] = jnp.sum(gp_ref[:, 2 * D :], axis=0, keepdims=True)

    flat_ref[:, BIAS_ROW:, :] = jnp.zeros((BLOCKS, FIRST_ROWS - BIAS_ROW, LANES), F32)
    flat_ref[:, BIAS_ROW, :] = collect(vsum[:, GAINS:], BIAS_PART, BIASES)
    flat_ref[:, GAIN_ROW, :] = collect(vsum[:, :GAINS], GAIN_PART, GAINS)

    def pairs(p, carry):
        rows = pl.ds(pl.multiple_of(p * 2 * STRIPE, 8), 2 * STRIPE)
        for t in range(QKV_TILES):
            scatter_rows(flat_ref, p, t, QKV_TILES, dwq[rows, t * LANES : (t + 1) * LANES])
        return carry

    lax.fori_loop(0, BLOCKS // 2, pairs, 0)
    pack(me, flat_ref, grads, 0, 0, FIRST_ROWS)


def near_shape(dims, kind):
    return pltpu.VMEM(dims, kind)


def call(kernel, swaps, outs, scratch, cost, *operands):
    specs = [pl.BlockSpec(memory_space=pltpu.SMEM)]
    specs += [pl.BlockSpec(memory_space=pltpu.VMEM)] * (len(operands) - 1)
    operands = [
        pltpu.with_memory_space_constraint(operand, pltpu.VMEM) if operand.ndim == 2
        or operand.shape[0] == 8 else operand
        for operand in operands
    ]
    return pl.pallas_call(
        functools.partial(kernel, swaps),
        out_shape=outs,
        in_specs=specs,
        out_specs=[pl.BlockSpec(memory_space=pltpu.VMEM)] * len(outs),
        scratch_shapes=scratch,
        compiler_params=pltpu.CompilerParams(vmem_limit_bytes=36 * 1024 * 1024),
        cost_estimate=pl.CostEstimate(flops=cost, transcendentals=0, bytes_accessed=4_000_000),
    )(*operands)


def attend(swaps, counts, images, pieces):
    outs = [
        near_shape((D, 3 * D), BF16),
        near_shape((1, GAINS + BIASES), F32),
        near_shape((ROWS, 3 * D), BF16),
        near_shape((ROWS, D), BF16),
    ]
    scratch = [
        pltpu.VMEM((BLOCKS, FIRST_ROWS, LANES), F32),
        pltpu.VMEM((ROWS, D), F32),
    ]
    return call(attend_kernel, swaps, outs, scratch, 5_000_000_000, counts, images, *pieces)


def piece_shapes(*split):
    return [near_shape((8, rows, LANES), BF16) for rows in split for _ in range(4)]


def mlp(swaps, counts, images, upstream, attended, vec, pieces):
    outs = [
        jax.ShapeDtypeStruct((IMGS, SEQ, D), BF16),
        near_shape((ROWS, D), F32),
        near_shape((1, GAINS + BIASES), F32),
        near_shape((D, D), BF16),
    ] + piece_shapes(*SUM_SPLIT)
    scratch = [
        pltpu.VMEM((BLOCKS, SECOND_ROWS, LANES), F32),
        pltpu.VMEM((CHUNKS, D, D), BF16),
        pltpu.VMEM((CHUNKS, D, D), BF16),
        pltpu.VMEM((CHUNKS, D, D), F32),
        pltpu.VMEM((CHUNKS, D, D), F32),
        pltpu.VMEM((D, D), F32),
        pltpu.VMEM((CHUNKS, 1, D), F32),
        pltpu.VMEM((CHUNKS, 1, D), F32),
        pltpu.VMEM((ROWS, D), F32),
        pltpu.VMEM((ROWS, D), BF16),
        pltpu.VMEM((ROWS, D), BF16),
        pltpu.VMEM((ROWS, D), F32),
        pltpu.VMEM((ROWS, D), F32),
    ]
    return call(
        mlp_kernel, swaps, outs, scratch, 8_000_000_000,
        counts, images, upstream, attended, vec, *pieces,
    )


def back(swaps, counts, images, qkv, grad_mid, w_qkv, w_out, vec, vec_grad):
    outs = [jax.ShapeDtypeStruct((IMGS, SEQ, D), BF16)] + piece_shapes(FIRST_ROWS)
    scratch = [
        pltpu.VMEM((BLOCKS, FIRST_ROWS, LANES), F32),
        pltpu.VMEM((ROWS, D), F32),
        pltpu.VMEM((ROWS, D), BF16),
        pltpu.VMEM((ROWS, 3 * D), F32),
        pltpu.VMEM((ROWS, 3 * D), BF16),
        pltpu.VMEM((D, 3 * D), F32),
        pltpu.VMEM((1, GAINS + BIASES), F32),
    ]
    return call(
        back_kernel, swaps, outs, scratch, 6_000_000_000,
        counts, images, qkv, grad_mid, w_qkv, w_out, vec, vec_grad,
    )


def exchange(value, mask):
    return lax.ppermute(value, AXES, [(i, i ^ mask) for i in range(BLOCKS)])


def gather_line(block):
    line = [block]
    for mask in LINE:
        line.append(exchange(block, mask))
    held = jnp.stack(line)
    held = jnp.concatenate([held, exchange(held, Y_BIT)])
    other = exchange(held, X_BIT)
    core = exchange(held, CORE_BIT)
    last = exchange(other, CORE_BIT)
    return [held, other, core, last]


def reduce_line(pieces):
    keep, keep_far, send, send_far = pieces
    from_core = exchange(send_far, CORE_BIT)
    far_sum = keep_far.astype(F32) + from_core.astype(F32)
    crossed = exchange(far_sum.astype(BF16), X_BIT)
    from_core = exchange(send, CORE_BIT)
    held = keep.astype(F32) + from_core.astype(F32) + crossed.astype(F32)
    crossed = exchange(held[4:].astype(BF16), Y_BIT)
    return sum_line(held[:4] + crossed.astype(F32))


def sum_line(line):
    total = line[0]
    for step, mask in enumerate(LINE):
        crossed = exchange(line[step + 1].astype(BF16), mask)
        total = total + crossed.astype(F32)
    return total


def gather_blocks(block, split):
    line = [block]
    for mask in LINE:
        line.append(exchange(block, mask))
    colors = []
    for color, (near, far) in enumerate(((Y_BIT, X_BIT), (X_BIT, Y_BIT))):
        part = slice(0, split[0]) if color == 0 else slice(split[0], None)
        first = jnp.stack([piece[part] for piece in line])
        colors.append((first, exchange(first, near), far))
    pieces = []
    for first, second, far in colors:
        plane = jnp.concatenate([first, second])
        other = exchange(plane, far)
        core = exchange(plane, CORE_BIT)
        last = exchange(other, CORE_BIT)
        pieces += [plane, other, core, last]
    return pieces


def reduce_blocks(pieces, ready):
    done = []
    for color, (near, far) in enumerate(((Y_BIT, X_BIT), (X_BIT, Y_BIT))):
        keep, keep_far, send, send_far = pieces[4 * color : 4 * color + 4]
        from_core = exchange(send_far, CORE_BIT)
        far_sum = keep_far.astype(F32) + from_core.astype(F32)
        crossed = exchange(far_sum.astype(BF16), far)
        from_core = exchange(send, CORE_BIT)
        plane = keep.astype(F32) + from_core.astype(F32) + crossed.astype(F32)
        crossed = exchange(plane[4:].astype(BF16), near)
        if color == 1:
            ready = [with_layout_constraint(value, TOKEN_MAJOR) for value in ready]
            crossed, *ready = lax.optimization_barrier((crossed, *ready))
        done.append(plane[:4] + crossed.astype(F32))
    line = jnp.concatenate(done, axis=1)
    return sum_line(line), ready


def ordered_pieces(whole, split):
    cube = whole.reshape(2, 2, 4, 2, -1, LANES)
    if len(split) == 1:
        pieces = [cube[x, core].swapaxes(0, 1) for core in range(2) for x in range(2)]
        return [piece.reshape((8,) + piece.shape[2:]) for piece in pieces]
    near, far = cube[..., : split[0], :], cube[..., split[0] :, :]
    pieces = [near[x, core].swapaxes(0, 1) for core in range(2) for x in range(2)]
    pieces += [far[:, core, :, y] for core in range(2) for y in range(2)]
    return [piece.reshape((8,) + piece.shape[2:]) for piece in pieces]


def blocks_of_pieces(pieces):
    first = jnp.stack(pieces[:4]).reshape(2, 2, 2, 4, -1, LANES)
    if len(pieces) == 4:
        return first.transpose(1, 0, 3, 2, 4, 5).reshape(BLOCKS, -1, LANES)
    second = jnp.stack(pieces[4:]).reshape(2, 2, 2, 4, -1, LANES)
    first = first.transpose(1, 0, 3, 2, 4, 5)
    second = second.transpose(2, 0, 3, 1, 4, 5)
    return jnp.concatenate([first, second], axis=4).reshape(BLOCKS, -1, LANES)


def block_rows(flat, rows):
    flat = flat.reshape(flat.shape[:-1] + (-1,))
    short = rows * LANES - flat.shape[-1]
    if short:
        flat = jnp.pad(flat, [(0, 0)] * (flat.ndim - 1) + [(0, short)])
    return flat.reshape(flat.shape[:-1] + (rows, LANES))


def padded_rows(parts, rows):
    short = rows - sum(part.shape[-2] for part in parts)
    filler = jnp.zeros(parts[0].shape[:-2] + (short, LANES), parts[0].dtype)
    return jnp.concatenate([*parts, filler], axis=-2)


def build_first(qkv, gains, biases):
    parts = [block_rows(qkv, QKV_ROWS), block_rows(biases, 1), block_rows(gains, 1)]
    return padded_rows(parts, FIRST_ROWS)


def build_second(out, fc1, fc2):
    parts = [block_rows(fc1, FC_ROWS), block_rows(out, OUT_ROWS), block_rows(fc2, FC_ROWS)]
    return padded_rows(parts, SECOND_ROWS)


def flat_rows(block, start, rows):
    return block[..., start : start + rows, :].reshape(block.shape[:-2] + (-1,))


def split_blocks(first, second):
    return (
        flat_rows(first, 0, QKV_ROWS),
        flat_rows(second, OUT_START, OUT_ROWS),
        flat_rows(second, 0, FC_ROWS),
        flat_rows(second, FC2_START, FC_ROWS),
        first[..., GAIN_ROW, :GAIN_PART],
        first[..., BIAS_ROW, :BIAS_PART],
    )


def adam_update(weight, gradient, moment_one, moment_two, step_rate, decayed):
    first_new = BETA_ONE * moment_one + (1.0 - BETA_ONE) * gradient
    second_new = BETA_TWO * moment_two + (1.0 - BETA_TWO) * gradient * gradient
    first_hat = first_new / (1.0 - BETA_ONE**ADAM_STEP)
    second_hat = second_new / (1.0 - BETA_TWO**ADAM_STEP)
    change = first_hat / (jnp.sqrt(second_hat) + ADAM_EPS)
    if decayed:
        change = change + DECAY_RATE * weight
    return (weight - step_rate * change, first_new, second_new)


def device_step(devices, images, counts, upstream, *state):
    masters, firsts, seconds = state[:6], state[6:12], state[12:18]
    swaps = devices == BLOCKS
    if swaps:
        qkv, out, fc1, fc2, gains, biases = masters
        first = gather_line(build_first(qkv, gains, biases).astype(BF16))
        second = gather_blocks(build_second(out, fc1, fc2).astype(BF16), GATHER_SPLIT)
    else:
        qkv, out, fc1, fc2, gains, biases = [
            lax.all_gather(part.astype(BF16), AXES, axis=0, tiled=True).reshape(BLOCKS, -1)
            for part in masters
        ]
        first = ordered_pieces(build_first(qkv, gains, biases), (FIRST_ROWS,))
        second = ordered_pieces(build_second(out, fc1, fc2), GATHER_SPLIT)
    w_qkv, vec, qkv, attended = attend(swaps, counts, images, first)
    block_out, grad_mid, vec_grad, w_out, *second_grads = mlp(
        swaps, counts, images, upstream, attended, vec, second
    )
    images_grad, *first_grads = back(
        swaps, counts, images, qkv, grad_mid, w_qkv, w_out, vec, vec_grad
    )
    if swaps:
        second_sum, (block_out, images_grad) = reduce_blocks(second_grads, (block_out, images_grad))
        first_sum = reduce_line(first_grads)
        owned = split_blocks(first_sum, second_sum)
    else:
        owned = tuple(
            lax.psum_scatter(part.reshape(-1), AXES, scatter_dimension=0, tiled=True)
            for part in split_blocks(
                blocks_of_pieces(first_grads).astype(F32),
                blocks_of_pieces(second_grads).astype(F32),
            )
        )
    updates = [
        adam_update(masters[p], owned[p], firsts[p], seconds[p], RATES[p], DECAYED[p])
        for p in range(6)
    ]
    return (
        block_out,
        images_grad,
        *owned,
        *(update[0] for update in updates),
        *(update[1] for update in updates),
        *(update[2] for update in updates),
    )


def solution(mesh):
    devices = math.prod(mesh.shape.values())
    slots = P(AXES, None, None)
    flat = P(AXES)

    def step(*args):
        return device_step(devices, *args)

    return jax.shard_map(
        step,
        mesh=mesh,
        in_specs=(slots, P(), slots) + (flat,) * 18,
        out_specs=(slots, slots) + (flat,) * 24,
        check_vma=False,
    )
```
